32 devices in a mesh: dp: 8 (over z, y), mp: 4 (over x, core).
Axes of the slice: x: 2, y: 2, z: 4, core: 2. Of those that a mesh axis runs over, the one named last changes fastest.
Arguments:
- states: bfloat16 [23040, 4096], P('dp', 'mp'), may hold values from -6 to 6
- proj: bfloat16 [4096, 128], P('mp'), may hold values from -0.09375 to 0.09375
- queries: bfloat16 [16384, 128], P(('dp', 'mp')), may hold values from -6 to 6
- lengths: int32 [128], P(('dp', 'mp')), may hold values from 1 to 180, 14400 in all
- slot_passage: int32 [8, 4, 8, 2], P('dp', 'mp'), may hold values from 0 to 3
- candidates: int32 [512, 8], P(('dp', 'mp')), may hold values from 0 to 15, all different within a row
- teacher: float32 [512, 8], P(('dp', 'mp')), may hold values from -8 to 8
Outputs:
- scores: float32 [512, 8], P(('dp', 'mp'))
- grad_proj: float32 [4096, 128], P('mp')
The draws below stay inside these ranges and needn't reach their ends.
Inputs may be any that keep to these rules, and one draw needn't show every extreme that they name: `slot_passage`: each entry names a passage of the sending device, counted within that device. The 8 candidates of a query are different slots.
All inputs are finite; a program needn't handle non-finite values. No bound on the sum of `lengths` on one device may be relied on, other than what follows from the above.
Results may differ from the reference program's by a relative error of at most 0.0072.
Values may be sent and summed in bfloat16 or wider, within the bound.
A program may use at most 128 MiB of HBM per device.

```python
import math
import jax
import jax.numpy as jnp
import numpy as np
from jax import lax

D = 4096
DIM = 128
LQ = 32
LP = 180
P_MP = 4
CAP = 2
Q_DEV = 16
SLOTS = 16
K = 8
QUERIES = 512
PASSAGES = 128
N_DP = 8
N_MP = 4


def with_ends(drawn, own_key, low, high):
    index_at = [jax.random.randint(jax.random.fold_in(own_key, axis), (), 0, length) for axis, length in enumerate(drawn.shape)]
    main_axis = drawn.shape.index(max(drawn.shape))
    neighbour = index_at[:main_axis] + [(index_at[main_axis] + 1) % drawn.shape[main_axis]] + index_at[main_axis + 1:]
    return drawn.at[tuple(index_at)].set(low).at[tuple(neighbour)].set(high)


def levels(stream_key, shape, pieces, least, high):
    loudness, own = 1.0, jax.random.fold_in(stream_key, 6)
    for axis_at, blocks in pieces:
        draws = jnp.exp(jax.random.uniform(jax.random.fold_in(own, axis_at), (blocks,), jnp.float32, least / len(pieces), high / len(pieces)))
        loudness = loudness * jnp.repeat(draws, shape[axis_at] // blocks).reshape([-1 if axis == axis_at else 1 for axis in range(len(shape))])
    return loudness


def distinct(stream_key, rows, amount, top, lift):
    order = jax.random.permutation(jax.random.fold_in(stream_key, 1), amount)
    pull = order
    for power in range(3):
        pull = pull * pull // amount
    pull = pull * lift // amount
    lots = jax.random.randint(jax.random.fold_in(stream_key, 2), (rows, amount), 0, 4096) + pull
    fixed_rows = jax.random.permutation(jax.random.fold_in(stream_key, 3), rows)[jnp.arange(amount) % rows]
    lots = jnp.where(jnp.arange(rows)[:, None] == fixed_rows[None, :], 1 << 14, lots)
    merit = lots * amount + jnp.arange(amount)
    return lax.top_k(merit.astype(jnp.int32), top)[1].astype(jnp.int32)


def split_up(number_of, total, most, skew):
    loads = [(1 << 20) // math.isqrt(standing ** skew) + 1 for standing in range(2, number_of + 1)]
    spare, holding = total - most - (number_of - 1), [1] * (number_of - 1)
    while spare > 0:
        free = [i for i in range(number_of - 1) if holding[i] < most]
        whole, left = sum([loads[i] for i in free]), spare
        for i in free:
            addition = min(most - holding[i], max(1, left * loads[i] // whole), spare)
            holding[i] = holding[i] + addition
            spare = spare - addition
    return np.array([most] + holding)


def ragged_sizes(key, count, total, limit, lean):
    if count == 2:
        one = jax.random.randint(key, (), max(1, total - limit), min(limit, total - 1) + 1)
        return jnp.stack([one, total - one])
    sizes = jnp.asarray(split_up(count, total, limit, lean), jnp.int32)
    pairs = (count - 1) // 2
    source_of, taker = sizes[1:1 + 2 * pairs:2], sizes[2:2 + 2 * pairs:2]
    room = jnp.minimum(source_of - 1, limit - taker)
    passed = jax.random.randint(jax.random.fold_in(key, 1), (pairs,), 0, 1 << 20) % (room + 1)
    sizes = sizes.at[1:1 + 2 * pairs:2].set(source_of - passed).at[2:2 + 2 * pairs:2].set(taker + passed)
    return sizes[jax.random.permutation(jax.random.fold_in(key, 2), count)]


def gaussian(key, shape, spread, reach, pieces=(), held_as=jnp.bfloat16):
    drawn = spread * jax.random.normal(key, shape, jnp.float32)
    if pieces:
        drawn = drawn * levels(key, shape, pieces, -0.22, 0.18)
    return jnp.clip(drawn, -reach, reach).astype(held_as)


def setup_inputs(seed: int = 0) -> dict:
    keys = jax.random.split(jax.random.key(seed), 8)
    return {
        "states": gaussian(keys[0], (PASSAGES * LP, D), 1.0, 6.0, ((0, 8), (1, 4))),
        "proj": gaussian(keys[1], (D, DIM), D ** -0.5, 0.09375, ((0, 4),)),
        "queries": gaussian(keys[2], (QUERIES * LQ, DIM), 1.0, 6.0, ((0, 32),)),
        "lengths": ragged_sizes(keys[3], PASSAGES, PASSAGES * LP * 5 // 8, LP, 2).astype(jnp.int32),
        "slot_passage": with_ends(jax.random.randint(keys[4], (N_DP, N_MP, N_DP, CAP), 0, P_MP), jax.random.fold_in(keys[4], 1), 0, P_MP - 1).astype(jnp.int32),
        "candidates": distinct(keys[5], QUERIES, SLOTS, K, 8192),
        "teacher": gaussian(keys[6], (QUERIES, K), 2.0, 8.0, ((0, 32),), jnp.float32),
    }


smooth_tau = 0.0625
loss_scale = 1024.0
norm_eps = 1e-06

def unit_rows(values):
    scales = jnp.sqrt(lax.optimization_barrier(jnp.sum(values * values, axis=-1, keepdims=True)) + norm_eps)
    return (values / scales, scales)

def slot_scores(query_rows, slot_vectors, slot_lengths):
    number = slot_vectors.shape[0]
    flat_slots = slot_vectors.reshape(number * LP, DIM)
    similar = lax.dot_general(query_rows, flat_slots, (((1,), (1,)), ((), ())), preferred_element_type=jnp.float32)
    similar = similar.reshape(-1, LQ, number, LP)
    positions = jnp.arange(LP, dtype=jnp.float32)
    active = (positions[None, :] < slot_lengths.astype(jnp.float32)[:, None]).astype(jnp.float32)
    powered = jnp.exp(similar / smooth_tau) * active
    totals_here = lax.optimization_barrier(jnp.sum(powered, axis=-1))
    slot_total = smooth_tau * lax.optimization_barrier(jnp.sum(jnp.log(totals_here), axis=1))
    return (slot_total, powered / totals_here[..., None])

def kl_grads(slot_total, chosen, teacher):
    number = slot_total.shape[1]
    choose = (chosen[:, :, None] == jnp.arange(number, dtype=jnp.int32)[None, None, :]).astype(jnp.float32)
    picked_scores = lax.optimization_barrier(jnp.sum(slot_total[:, None, :] * choose, axis=-1))
    student = jnp.exp(picked_scores)
    student = student / lax.optimization_barrier(jnp.sum(student, axis=-1, keepdims=True))
    target = jnp.exp(teacher)
    target = target / lax.optimization_barrier(jnp.sum(target, axis=-1, keepdims=True))
    score_grad = loss_scale * (student - target)
    slot_grad = lax.optimization_barrier(jnp.sum(score_grad[:, :, None] * choose, axis=1))
    return (picked_scores, slot_grad)

def reference(states, proj, queries, lengths, slot_passage, candidates, teacher):
    embedded = jnp.dot(states, proj, preferred_element_type=jnp.float32)
    unit_vals, row_norms = unit_rows(embedded)
    passages = unit_vals.astype(jnp.bfloat16).reshape(PASSAGES, LP, DIM)
    query_unit, query_norms = unit_rows(queries.astype(jnp.float32))
    query_vectors = query_unit.astype(jnp.bfloat16)
    groups = N_DP * N_MP
    slot_count = N_DP * CAP
    ordered = jnp.transpose(slot_passage, (2, 1, 0, 3)).astype(jnp.int32)
    sender = jnp.arange(N_DP, dtype=jnp.int32)[None, None, :, None]
    column = jnp.arange(N_MP, dtype=jnp.int32)[None, :, None, None]
    slot_global = ((sender * N_MP + column) * P_MP + ordered).reshape(groups, slot_count)
    inputs_all = (query_vectors.reshape(groups, Q_DEV * LQ, DIM), candidates.reshape(groups, Q_DEV, K), teacher.reshape(groups, Q_DEV, K), slot_global)

    def step_group(carried, inputs):
        group_queries, group_cands, group_teacher, group_slots = inputs
        slot_total, weights = slot_scores(group_queries, passages[group_slots], lengths[group_slots])
        picked_scores, slot_grad = kl_grads(slot_total, group_cands, group_teacher)
        coefficient = (weights * slot_grad[:, None, :, None]).astype(jnp.bfloat16).reshape(Q_DEV * LQ, slot_count * LP)
        back_rows = lax.dot_general(coefficient, group_queries, (((0,), (0,)), ((), ())), preferred_element_type=jnp.float32)
        return (carried.at[group_slots].add(back_rows.reshape(slot_count, LP, DIM)), picked_scores)
    vector_grad, scores = lax.scan(step_group, jnp.zeros((PASSAGES, LP, DIM), jnp.float32), inputs_all)
    vector_grad = vector_grad.reshape(PASSAGES * LP, DIM)
    along_unit = lax.optimization_barrier(jnp.sum(unit_vals * vector_grad, axis=-1, keepdims=True))
    embed_grad = ((vector_grad - unit_vals * along_unit) / row_norms).astype(jnp.bfloat16)
    grad_proj = lax.dot_general(states, embed_grad, (((0,), (0,)), ((), ())), preferred_element_type=jnp.float32)
    return (scores.reshape(QUERIES, K), grad_proj)
```

```python
import functools

import jax
import jax.numpy as jnp
from jax import lax
from jax.experimental import pallas as pl
from jax.experimental.pallas import tpu as pltpu
from jax.sharding import PartitionSpec as P

DIM = 128
LQ = 32
LP = 180
LANES = 128
PARTS = 2
ADD_CUTS = 2
ADD_UNROLL = 4
LOG2E = 1.4426950408889634
DEAD = -1e30

smooth_tau = 0.0625
loss_scale = 1024.0
norm_eps = 1e-06

MESH = pl.DeviceIdType.MESH
HIGHEST = lax.Precision.HIGHEST
F32 = jnp.float32
BF16 = jnp.bfloat16


def remote(src, dst, send, recv, where):
    return pltpu.make_async_remote_copy(
        src_ref=src, dst_ref=dst, send_sem=send, recv_sem=recv, device_id=where, device_id_type=MESH
    )


def kernel(
    sizes,
    lengths,
    selected,
    states,
    proj,
    queries,
    candidates,
    teacher,
    scores_out,
    grad_out,
    held,
    proj_ref,
    pair_send,
    pair_recv,
    chip_part,
    chip_send,
    chip_recv,
    embed,
    unit_ref,
    norm_ref,
    bias_ref,
    vectors,
    raw_queries,
    query_vecs,
    powered,
    totals,
    scale_ref,
    own_scores,
    marks,
    marks_by_slot,
    slot_scores,
    shares,
    backs,
    grad_rows,
    embed_grads,
    acc,
    part_send,
    part_recv,
    final,
    load_sem,
    own_sem,
    proj_sem,
    left_sem,
    pair_sem,
    chip_sem,
    row_sem,
    side_sem,
    mark_sem,
    share_sem,
    score_sem,
    gpair_sem,
    gchip_sem,
    part_sem,
    final_sem,
    out_sem,
):
    n_dp, n_mp, held_count, cap, n_q = sizes
    chips = n_mp // 2
    sides = 2 if n_dp % 2 == 0 else 1
    lines = n_dp // sides
    rows = held_count * LP
    padded = vectors.shape[1]
    slots = n_dp * cap
    dp = lax.axis_index("dp")
    mp = lax.axis_index("mp")
    chip, core = mp // 2, mp % 2
    other = 1 - core
    line, side = dp // sides, dp % sides

    barrier = pltpu.get_barrier_semaphore()
    for d in range(1, n_dp):
        pl.semaphore_signal(
            barrier, inc=1, device_id={"dp": (dp + d) % n_dp}, device_id_type=MESH
        )
    for d in range(1, n_mp):
        pl.semaphore_signal(
            barrier, inc=1, device_id={"mp": (mp + d) % n_mp}, device_id_type=MESH
        )

    def mp_at(dx, which):
        return ((chip + dx) % chips) * 2 + which

    proj_load = pltpu.make_async_copy(proj, proj_ref, proj_sem)
    proj_load.start()
    order = []
    for dx in range(1, chips):
        order += [mp_at(dx, other), mp_at(dx, core)]
    order += [mp_at(0, other), mp_at(0, core)]
    loads = []
    for at, block in enumerate(order):
        copy = pltpu.make_async_copy(states.at[block], held.at[block], load_sem.at[at])
        copy.start()
        loads.append(copy)
    own_load = pltpu.make_async_copy(queries, raw_queries.at[dp], own_sem)
    own_load.start()

    pending = []

    def start(copy):
        copy.start()
        pending.append(copy)
        return copy

    half = queries.shape[0] // PARTS

    def rows_of(part):
        return pl.ds(part * half, half)

    def step_right(source, part, own=False):
        there = raw_queries.at[source, rows_of(part)]
        return remote(
            queries.at[rows_of(part)] if own else there,
            there,
            row_sem.at[0, source, part],
            row_sem.at[1, source, part],
            {"dp": jnp.minimum(line + 1, lines - 1) * sides + side},
        )

    def step_left(source, part, own=False):
        there = raw_queries.at[source, rows_of(part)]
        return remote(
            queries.at[rows_of(part)] if own else there,
            there,
            left_sem.at[source, part],
            row_sem.at[1, source, part],
            {"dp": jnp.maximum(line - 1, 0) * sides + side},
        )

    def step_side(source, part, own=False):
        there = raw_queries.at[source, rows_of(part)]
        return remote(
            queries.at[rows_of(part)] if own else there,
            there,
            side_sem.at[0, source, part],
            side_sem.at[1, source, part],
            {"dp": line * sides + (1 - side)},
        )

    pl.semaphore_wait(barrier, n_dp + n_mp - 2)
    for part in range(PARTS):

        @pl.when(line < lines - 1)
        def _():
            step_right(dp, part, True).start()

        @pl.when(line > 0)
        def _():
            step_left(dp, part, True).start()

        if sides == 2:
            step_side(dp, part, True).start()

    partner = {"mp": mp_at(0, other)}
    pair_copies, chip_copies = {}, {}

    def send_pair(dx):
        pair_copies[dx] = start(
            remote(
                pair_send.at[dx],
                pair_recv.at[dx],
                pair_sem.at[0, dx],
                pair_sem.at[1, dx],
                partner,
            )
        )

    def partial(at):
        loads[at].wait()
        return jnp.dot(held[order[at]], proj_ref[...], preferred_element_type=F32)

    proj_load.wait()
    for dx in range(1, chips):
        pair_send[dx] = partial(2 * dx - 2)
        send_pair(dx)
        chip_part[dx] = partial(2 * dx - 1)
    for dx in range(1, chips):
        pair_copies[dx].wait_recv()
        chip_send[dx] = (chip_part[dx] + pair_recv[dx]).astype(BF16)
        chip_copies[dx] = start(
            remote(
                chip_send.at[dx],
                chip_recv.at[dx],
                chip_sem.at[0, dx],
                chip_sem.at[1, dx],
                {"mp": mp_at(dx, core)},
            )
        )
    pair_send[0] = partial(n_mp - 2)
    send_pair(0)
    embed[...] = partial(n_mp - 1)

    def hop(k):
        for part in range(PARTS):

            @pl.when(line >= k)
            def _():
                source = (line - k) * sides + side
                copy = step_right(source, part)
                copy.wait_recv()

                @pl.when(line < lines - 1)
                def _():
                    copy.start()

                if sides == 2:
                    step_side(source, part).start()

            @pl.when(line + k < lines)
            def _():
                source = (line + k) * sides + side
                copy = step_left(source, part)
                copy.wait_recv()

                @pl.when(line > 0)
                def _():
                    copy.start()

                if sides == 2:
                    step_side(source, part).start()

    def prepare(r):
        values = raw_queries[r].astype(F32)
        query_vecs[r] = (
            values / jnp.sqrt(jnp.sum(values * values, axis=-1, keepdims=True) + norm_eps)
        ).astype(BF16)

    def score(r):
        rows_r = query_vecs[r]
        for c in range(cap):
            pair = r * cap + c
            p = selected[c, r]
            similar = lax.dot_general(
                vectors[p], rows_r, (((1,), (1,)), ((), ())), preferred_element_type=F32
            )
            dead = jnp.concatenate([bias_ref[p]] * (similar.shape[1] // LANES), axis=1)
            grown = jnp.exp2(similar * (LOG2E / smooth_tau) + dead)
            powered[pair] = grown
            totals[pl.ds(c * n_dp + r, 1), :] = jnp.sum(grown, axis=0, keepdims=True)

    def along_line(k, body):
        def one(j, carry):
            at = line - k + 2 * k * j

            @pl.when((at >= 0) & (at < lines))
            def _():
                body(at)

            return carry

        lax.fori_loop(0, 1 if k == 0 else 2, one, 0)

    def line_prepare(k):
        along_line(k, lambda at: prepare(at * sides + side))

    def side_arrives(k):
        def body(at):
            source = at * sides + 1 - side
            for part in range(PARTS):
                step_side(source, part).wait_recv()
            prepare(source)
            score(source)

        if sides == 2:
            along_line(k, body)

    hop(1)

    target = jnp.exp(teacher[...])
    target = target / jnp.sum(target, axis=0, keepdims=True)
    chosen = candidates[...]
    slot_row = lax.broadcasted_iota(jnp.int32, (slots, n_q), 0)
    by_slot = jnp.full((slots, n_q), -1.0, F32)
    for k in range(chosen.shape[0]):
        by_slot = jnp.where(slot_row == chosen[k : k + 1, :], target[k : k + 1, :], by_slot)
    marks[dp] = jnp.full((slots, LANES), -1.0, F32)
    marks[dp, :, 0:n_q] = by_slot
    mark_copies = []
    for d in range(1, n_dp):
        there = {"dp": (dp + d) % n_dp}
        mark_copies.append(
            start(
                remote(marks.at[dp], marks.at[dp], mark_sem.at[0, d], mark_sem.at[1, d], there)
            )
        )
    row_at = lax.broadcasted_iota(jnp.int32, (padded, LANES), 0)
    for p in range(held_count):
        bias_ref[p] = jnp.where(row_at < lengths[p], 0.0, DEAD)
    pair_copies[0].wait_recv()
    embed[...] += pair_recv[0]
    own_load.wait()
    line_prepare(0)
    for k in range(2, lines):
        hop(k)
        line_prepare(k - 1)

    total = embed[...]
    for dx in range(1, chips):
        chip_copies[dx].wait_recv()
        total = total + chip_recv[dx].astype(F32)
    embed[...] = total
    for p in range(held_count):
        piece = embed[p * LP : (p + 1) * LP, :]
        norms = jnp.sqrt(jnp.sum(piece * piece, axis=-1, keepdims=True) + norm_eps)
        units = piece / norms
        unit_ref[p, 0:LP, :] = units
        unit_ref[p, LP:padded, :] = jnp.zeros((padded - LP, DIM), F32)
        norm_ref[p, 0:LP, :] = jnp.broadcast_to(1.0 / norms, (LP, DIM))
        vectors[p] = unit_ref[p].astype(BF16)

    if lines > 1:
        line_prepare(lines - 1)

    def score_line(at, carry):
        score(at * sides + side)
        return carry

    lax.fori_loop(0, lines, score_line, 0)
    for copy in mark_copies:
        copy.wait_recv()
    for v in range(slots):
        s, c = v // cap, v % cap
        marks_by_slot[s, c * n_dp : (c + 1) * n_dp, :] = marks[:, v, :]
    for k in range(lines):
        side_arrives(k)

    spread = (
        lax.broadcasted_iota(jnp.int32, (n_q * LQ, LANES), 0) // LQ
        == lax.broadcasted_iota(jnp.int32, (n_q * LQ, LANES), 1)
    ).astype(F32)
    sums = totals[...]
    own_slots = smooth_tau * jnp.dot(
        jnp.log(sums), spread, precision=HIGHEST, preferred_element_type=F32
    )
    own_marks = marks_by_slot[dp]
    student = jnp.where(own_marks >= 0.0, jnp.exp(own_slots), 0.0)
    mine = student[0:n_dp, :]
    for c in range(1, cap):
        mine = mine + student[c * n_dp : (c + 1) * n_dp, :]
    shares[dp] = mine
    share_copies, score_copies = [], []
    for d in range(1, n_dp):
        there = {"dp": (dp + d) % n_dp}
        share_copies.append(
            start(
                remote(
                    shares.at[dp], shares.at[dp], share_sem.at[0, d], share_sem.at[1, d], there
                )
            )
        )
    slot_scores[dp] = own_slots
    for d in range(1, n_dp):
        there = {"dp": (dp + d) % n_dp}
        score_copies.append(
            start(
                remote(
                    slot_scores.at[dp],
                    slot_scores.at[dp],
                    score_sem.at[0, d],
                    score_sem.at[1, d],
                    there,
                )
            )
        )
    for copy in share_copies:
        copy.wait_recv()

    whole = jnp.sum(shares[...], axis=0)
    whole = jnp.concatenate([whole] * cap, axis=0)
    slot_grad = jnp.where(own_marks >= 0.0, loss_scale * (student / whole - own_marks), 0.0)
    scale_ref[...] = (
        lax.dot_general(
            slot_grad,
            spread,
            (((1,), (1,)), ((), ())),
            precision=HIGHEST,
            preferred_element_type=F32,
        )
        / sums
    )

    def back(r, carry):
        rows_r = query_vecs[r]
        for c in range(cap):
            pair = r * cap + c
            coefficient = (powered[pair] * scale_ref[pl.ds(c * n_dp + r, 1), :]).astype(BF16)
            backs[pair] = jnp.dot(coefficient, rows_r, preferred_element_type=F32)
        return carry

    lax.fori_loop(0, n_dp, back, 0)

    def weigh(block):
        return lax.dot_general(
            embed_grads[block], held[block], (((0,), (0,)), ((), ())), preferred_element_type=F32
        )

    gchip_copies = [[] for _ in range(chips)]
    gpair_copies = [[] for _ in range(chips)]

    def forward(source, piece, dx):
        begin, size = piece
        cut = embed_grads.at[source, pl.ds(begin, size)]
        at = len(gpair_copies[dx])
        gpair_copies[dx].append(
            start(remote(cut, cut, gpair_sem.at[0, dx, at], gpair_sem.at[1, dx, at], partner))
        )

    pieces = []
    ready, sent_rows = 0, 0
    step = max(8, padded // ADD_CUTS)
    while ready < held_count:
        group = range(ready, min(ready + 2, held_count))
        grown_parts = [[] for _ in group]
        for cut in range(0, padded, step):

            def add(pair, sofar):
                piece = backs[pair, cut : cut + step, :]
                which = selected[pair % cap, pair // cap]
                return tuple(
                    now + jnp.where(which == p, piece, 0.0) for now, p in zip(sofar, group)
                )

            zero = jnp.zeros((step, DIM), F32)
            done = lax.fori_loop(0, slots, add, tuple(zero for _ in group), unroll=ADD_UNROLL)
            for keep, value in zip(grown_parts, done):
                keep.append(value)
        for keep, p in zip(grown_parts, group):
            for at, value in enumerate(keep):
                backs_sum = value
                begin = at * step
                size = min(step, LP - begin)
                units = unit_ref[p, begin : begin + size, :]
                along_unit = jnp.sum(units * backs_sum[0:size], axis=-1, keepdims=True)
                grad_rows[p * LP + begin : p * LP + begin + size, :] = (
                    backs_sum[0:size] - units * along_unit
                ) * norm_ref[p, begin : begin + size, :]
        ready = group[-1] + 1
        until = rows if ready == held_count else ready * LP // 16 * 16
        embed_grads[mp, sent_rows:until, :] = grad_rows[sent_rows:until, :].astype(BF16)
        piece = (sent_rows, until - sent_rows)
        pieces.append(piece)
        sent_rows = until
        cut = embed_grads.at[mp, pl.ds(piece[0], piece[1])]
        at = len(pieces) - 1
        for dx in range(1, chips):
            gchip_copies[dx].append(
                start(
                    remote(
                        cut,
                        cut,
                        gchip_sem.at[0, dx, at],
                        gchip_sem.at[1, dx, at],
                        {"mp": mp_at(dx, core)},
                    )
                )
            )
        forward(mp, piece, 0)

    acc[...] = weigh(mp)
    for copy in gpair_copies[0]:
        copy.wait_recv()
    acc[...] += weigh(mp_at(0, other))
    for dx in range(1, chips):
        source = ((chip - dx + chips) % chips) * 2 + core
        for at, piece in enumerate(pieces):
            gchip_copies[dx][at].wait_recv()
            forward(source, piece, dx)
        acc[...] += weigh(source)
    for dx in range(1, chips):
        for copy in gpair_copies[dx]:
            copy.wait_recv()
        acc[...] += weigh(((chip - dx + chips) % chips) * 2 + other)

    share = part_send.shape[1]
    part_send[...] = jnp.transpose(acc[...]).astype(BF16).reshape(n_dp, share, DIM)
    part_copies = []
    for d in range(1, n_dp):
        to = (dp + d) % n_dp
        part_copies.append(
            start(
                remote(
                    part_send.at[to],
                    part_recv.at[d],
                    part_sem.at[0, d],
                    part_sem.at[1, d],
                    {"dp": to},
                )
            )
        )
    whole = part_send[dp].astype(F32)
    for d in range(1, n_dp):
        part_copies[d - 1].wait_recv()
        whole = whole + part_recv[d].astype(F32)
    final[...] = whole.astype(BF16)
    final_copies = []
    for d in range(1, n_dp):
        final_copies.append(
            start(
                remote(
                    final,
                    grad_out.at[dp],
                    final_sem.at[0, d],
                    final_sem.at[1, d],
                    {"dp": (dp + d) % n_dp},
                )
            )
        )
    own_out = pltpu.make_async_copy(final, grad_out.at[dp], out_sem)
    own_out.start()

    for copy in score_copies:
        copy.wait_recv()
    for v in range(slots):
        s, c = v // cap, v % cap
        own_scores[v : v + 1, :] = slot_scores[s, pl.ds(c * n_dp + dp, 1), :]
    by_slot = own_scores[:, 0:n_q]
    for k in range(chosen.shape[0]):
        scores_out[k : k + 1, :] = jnp.sum(
            jnp.where(slot_row == chosen[k : k + 1, :], by_slot, 0.0), axis=0, keepdims=True
        )
    for copy in pending:
        copy.wait_send()

    def sent(at, carry):
        source = at * sides + side
        for part in range(PARTS):

            @pl.when((at <= line) & (line < lines - 1))
            def _():
                step_right(source, part).wait_send()

            @pl.when((at >= line) & (line > 0))
            def _():
                step_left(source, part).wait_send()

            if sides == 2:
                step_side(source, part).wait_send()
        return carry

    lax.fori_loop(0, lines, sent, 0)
    own_out.wait()
    for copy in final_copies:
        copy.wait_recv()


def finish(scores, grad, scores_out, grad_out):
    scores_out[...] = scores[...]
    grad_out[...] = grad[...].astype(F32)


def on_device(sizes, states, proj, queries, lengths, slot_passage, candidates, teacher):
    n_dp, n_mp, held_count, cap, n_q = sizes
    width = states.shape[1]
    rows = held_count * LP
    padded = (LP + 15) // 16 * 16
    pairs = n_dp * cap
    share = width // n_dp
    query_rows = n_q * LQ
    chips = n_mp // 2
    vmem = pl.BlockSpec(memory_space=pltpu.VMEM)
    smem = pl.BlockSpec(memory_space=pltpu.SMEM)
    hbm = pl.BlockSpec(memory_space=pl.ANY)
    scores, grad = pl.pallas_call(
        functools.partial(kernel, sizes),
        out_shape=(
            jax.ShapeDtypeStruct(candidates.shape[::-1], F32),
            jax.ShapeDtypeStruct((n_dp, share, DIM), BF16),
        ),
        in_specs=[smem, smem, hbm, hbm, hbm, vmem, vmem],
        out_specs=(vmem, hbm),
        scratch_shapes=[
            pltpu.VMEM((n_mp, rows, width), BF16),
            pltpu.VMEM((width, DIM), BF16),
            pltpu.VMEM((chips, rows, DIM), F32),
            pltpu.VMEM((chips, rows, DIM), F32),
            pltpu.VMEM((chips, rows, DIM), F32),
            pltpu.VMEM((chips, rows, DIM), BF16),
            pltpu.VMEM((chips, rows, DIM), BF16),
            pltpu.VMEM((rows, DIM), F32),
            pltpu.VMEM((held_count, padded, DIM), F32),
            pltpu.VMEM((held_count, padded, DIM), F32),
            pltpu.VMEM((held_count, padded, LANES), F32),
            pltpu.VMEM((held_count, padded, DIM), BF16),
            pltpu.VMEM((n_dp, query_rows, DIM), BF16),
            pltpu.VMEM((n_dp, query_rows, DIM), BF16),
            pltpu.VMEM((pairs, padded, query_rows), F32),
            pltpu.VMEM((pairs, query_rows), F32),
            pltpu.VMEM((pairs, query_rows), F32),
            pltpu.VMEM((pairs, LANES), F32),
            pltpu.VMEM((n_dp, pairs, LANES), F32),
            pltpu.VMEM((n_dp, pairs, LANES), F32),
            pltpu.VMEM((n_dp, pairs, LANES), F32),
            pltpu.VMEM((n_dp, n_dp, LANES), F32),
            pltpu.VMEM((pairs, padded, DIM), F32),
            pltpu.VMEM((rows, DIM), F32),
            pltpu.VMEM((n_mp, rows, DIM), BF16),
            pltpu.VMEM((DIM, width), F32),
            pltpu.VMEM((n_dp, share, DIM), BF16),
            pltpu.VMEM((n_dp, share, DIM), BF16),
            pltpu.VMEM((share, DIM), BF16),
            pltpu.SemaphoreType.DMA((n_mp,)),
            pltpu.SemaphoreType.DMA,
            pltpu.SemaphoreType.DMA,
            pltpu.SemaphoreType.DMA((n_dp, PARTS)),
            pltpu.SemaphoreType.DMA((2, chips)),
            pltpu.SemaphoreType.DMA((2, chips)),
            pltpu.SemaphoreType.DMA((2, n_dp, PARTS)),
            pltpu.SemaphoreType.DMA((2, n_dp, PARTS)),
            pltpu.SemaphoreType.DMA((2, n_dp)),
            pltpu.SemaphoreType.DMA((2, n_dp)),
            pltpu.SemaphoreType.DMA((2, n_dp)),
            pltpu.SemaphoreType.DMA((2, chips, held_count)),
            pltpu.SemaphoreType.DMA((2, chips, held_count)),
            pltpu.SemaphoreType.DMA((2, n_dp)),
            pltpu.SemaphoreType.DMA((2, n_dp)),
            pltpu.SemaphoreType.DMA,
        ],
        compiler_params=pltpu.CompilerParams(
            collective_id=0, has_side_effects=True, vmem_limit_bytes=62 * 1024 * 1024
        ),
    )(
        lengths,
        slot_passage.reshape(n_dp, cap).T,
        states.reshape(n_mp, rows, width),
        proj,
        queries,
        candidates.T,
        teacher.T,
    )
    scores, grad = pl.pallas_call(
        finish,
        out_shape=(
            jax.ShapeDtypeStruct(scores.shape, F32),
            jax.ShapeDtypeStruct((width, DIM), F32),
        ),
        in_specs=[vmem, vmem],
        out_specs=(vmem, vmem),
    )(scores, grad.reshape(width, DIM))
    return scores.T, grad


def solution(mesh):
    n_dp, n_mp = mesh.shape["dp"], mesh.shape["mp"]

    def whole(states, proj, queries, lengths, slot_passage, candidates, teacher):
        devices = n_dp * n_mp
        sizes = (
            n_dp,
            n_mp,
            lengths.shape[0] // devices,
            slot_passage.shape[3],
            candidates.shape[0] // devices,
        )
        return jax.shard_map(
            functools.partial(on_device, sizes),
            mesh=mesh,
            in_specs=(
                P("dp", "mp"),
                P("mp", None),
                P(("dp", "mp"), None),
                P(("dp", "mp")),
                P("dp", "mp", None, None),
                P(("dp", "mp"), None),
                P(("dp", "mp"), None),
            ),
            out_specs=(P(("dp", "mp"), None), P("mp", None)),
            check_vma=False,
        )(states, proj, queries, lengths, slot_passage, candidates, teacher)

    return whole
```

```python
import functools

import jax
import jax.numpy as jnp
from jax import lax
from jax.experimental import pallas as pl
from jax.experimental.pallas import tpu as pltpu
from jax.sharding import PartitionSpec as P

DIM = 128
LQ = 32
LP = 180
LANES = 128
PARTS = 2
ADD_CUTS = 2
ADD_UNROLL = 4
LOG2E = 1.4426950408889634
DEAD = -1e30

smooth_tau = 0.0625
loss_scale = 1024.0
norm_eps = 1e-06

MESH = pl.DeviceIdType.MESH
HIGHEST = lax.Precision.HIGHEST
F32 = jnp.float32
BF16 = jnp.bfloat16


def remote(src, dst, send, recv, where):
    return pltpu.make_async_remote_copy(
        src_ref=src, dst_ref=dst, send_sem=send, recv_sem=recv, device_id=where, device_id_type=MESH
    )


def kernel(
    sizes,
    lengths,
    selected,
    states,
    proj,
    queries,
    candidates,
    teacher,
    scores_out,
    grad_out,
    held,
    proj_ref,
    pair_send,
    pair_recv,
    chip_part,
    chip_send,
    chip_recv,
    embed,
    unit_ref,
    norm_ref,
    bias_ref,
    vectors,
    raw_queries,
    query_vecs,
    powered,
    totals,
    scale_ref,
    own_scores,
    marks,
    marks_by_slot,
    slot_scores,
    shares,
    backs,
    grad_rows,
    embed_grads,
    acc,
    part_send,
    part_recv,
    final,
    load_sem,
    own_sem,
    proj_sem,
    left_sem,
    pair_sem,
    chip_sem,
    row_sem,
    side_sem,
    mark_sem,
    share_sem,
    score_sem,
    gpair_sem,
    gchip_sem,
    part_sem,
    final_sem,
    out_sem,
    picked,
    scores_sem,
):
    n_dp, n_mp, held_count, cap, n_q = sizes
    chips = n_mp // 2
    sides = 2 if n_dp % 2 == 0 else 1
    lines = n_dp // sides
    rows = held_count * LP
    padded = vectors.shape[1]
    slots = n_dp * cap
    dp = lax.axis_index("dp")
    mp = lax.axis_index("mp")
    chip, core = mp // 2, mp % 2
    other = 1 - core
    line, side = dp // sides, dp % sides

    barrier = pltpu.get_barrier_semaphore()
    for d in range(1, n_dp):
        pl.semaphore_signal(
            barrier, inc=1, device_id={"dp": (dp + d) % n_dp}, device_id_type=MESH
        )
    for d in range(1, n_mp):
        pl.semaphore_signal(
            barrier, inc=1, device_id={"mp": (mp + d) % n_mp}, device_id_type=MESH
        )

    def mp_at(dx, which):
        return ((chip + dx) % chips) * 2 + which

    proj_load = pltpu.make_async_copy(proj, proj_ref, proj_sem)
    proj_load.start()
    order = []
    for dx in range(1, chips):
        order += [mp_at(dx, other), mp_at(dx, core)]
    order += [mp_at(0, other), mp_at(0, core)]
    loads = []
    for at, block in enumerate(order):
        copy = pltpu.make_async_copy(states.at[block], held.at[block], load_sem.at[at])
        copy.start()
        loads.append(copy)
    own_load = pltpu.make_async_copy(queries, raw_queries.at[dp], own_sem)
    own_load.start()

    pending = []

    def start(copy):
        copy.start()
        pending.append(copy)
        return copy

    half = queries.shape[0] // PARTS

    def rows_of(part):
        return pl.ds(part * half, half)

    def step_right(source, part, own=False):
        there = raw_queries.at[source, rows_of(part)]
        return remote(
            queries.at[rows_of(part)] if own else there,
            there,
            row_sem.at[0, source, part],
            row_sem.at[1, source, part],
            {"dp": jnp.minimum(line + 1, lines - 1) * sides + side},
        )

    def step_left(source, part, own=False):
        there = raw_queries.at[source, rows_of(part)]
        return remote(
            queries.at[rows_of(part)] if own else there,
            there,
            left_sem.at[source, part],
            row_sem.at[1, source, part],
            {"dp": jnp.maximum(line - 1, 0) * sides + side},
        )

    def step_side(source, part, own=False):
        there = raw_queries.at[source, rows_of(part)]
        return remote(
            queries.at[rows_of(part)] if own else there,
            there,
            side_sem.at[0, source, part],
            side_sem.at[1, source, part],
            {"dp": line * sides + (1 - side)},
        )

    pl.semaphore_wait(barrier, n_dp + n_mp - 2)
    for part in range(PARTS):

        @pl.when(line < lines - 1)
        def _():
            step_right(dp, part, True).start()

        @pl.when(line > 0)
        def _():
            step_left(dp, part, True).start()

        if sides == 2:
            step_side(dp, part, True).start()

    partner = {"mp": mp_at(0, other)}
    pair_copies, chip_copies = {}, {}

    def send_pair(dx):
        pair_copies[dx] = start(
            remote(
                pair_send.at[dx],
                pair_recv.at[dx],
                pair_sem.at[0, dx],
                pair_sem.at[1, dx],
                partner,
            )
        )

    def partial(at):
        loads[at].wait()
        return jnp.dot(held[order[at]], proj_ref[...], preferred_element_type=F32)

    proj_load.wait()
    for dx in range(1, chips):
        pair_send[dx] = partial(2 * dx - 2)
        send_pair(dx)
        chip_part[dx] = partial(2 * dx - 1)
    for dx in range(1, chips):
        pair_copies[dx].wait_recv()
        chip_send[dx] = (chip_part[dx] + pair_recv[dx]).astype(BF16)
        chip_copies[dx] = start(
            remote(
                chip_send.at[dx],
                chip_recv.at[dx],
                chip_sem.at[0, dx],
                chip_sem.at[1, dx],
                {"mp": mp_at(dx, core)},
            )
        )
    pair_send[0] = partial(n_mp - 2)
    send_pair(0)
    embed[...] = partial(n_mp - 1)

    def hop(k):
        for part in range(PARTS):

            @pl.when(line >= k)
            def _():
                source = (line - k) * sides + side
                copy = step_right(source, part)
                copy.wait_recv()

                @pl.when(line < lines - 1)
                def _():
                    copy.start()

                if sides == 2:
                    step_side(source, part).start()

            @pl.when(line + k < lines)
            def _():
                source = (line + k) * sides + side
                copy = step_left(source, part)
                copy.wait_recv()

                @pl.when(line > 0)
                def _():
                    copy.start()

                if sides == 2:
                    step_side(source, part).start()

    def prepare(r):
        values = raw_queries[r].astype(F32)
        query_vecs[r] = (
            values / jnp.sqrt(jnp.sum(values * values, axis=-1, keepdims=True) + norm_eps)
        ).astype(BF16)

    def score(r):
        rows_r = query_vecs[r]
        for c in range(cap):
            pair = r * cap + c
            p = selected[c, r]
            similar = lax.dot_general(
                vectors[p], rows_r, (((1,), (1,)), ((), ())), preferred_element_type=F32
            )
            dead = jnp.concatenate([bias_ref[p]] * (similar.shape[1] // LANES), axis=1)
            grown = jnp.exp2(similar * (LOG2E / smooth_tau) + dead)
            powered[pair] = grown
            totals[pl.ds(c * n_dp + r, 1), :] = jnp.sum(grown, axis=0, keepdims=True)

    def along_line(k, body):
        def one(j, carry):
            at = line - k + 2 * k * j

            @pl.when((at >= 0) & (at < lines))
            def _():
                body(at)

            return carry

        lax.fori_loop(0, 1 if k == 0 else 2, one, 0)

    def line_prepare(k):
        along_line(k, lambda at: prepare(at * sides + side))

    def side_arrives(k):
        def body(at):
            source = at * sides + 1 - side
            for part in range(PARTS):
                step_side(source, part).wait_recv()
            prepare(source)
            score(source)

        if sides == 2:
            along_line(k, body)

    hop(1)

    target = jnp.exp(teacher[...])
    target = target / jnp.sum(target, axis=0, keepdims=True)
    chosen = candidates[...]
    slot_row = lax.broadcasted_iota(jnp.int32, (slots, n_q), 0)
    by_slot = jnp.full((slots, n_q), -1.0, F32)
    for k in range(chosen.shape[0]):
        by_slot = jnp.where(slot_row == chosen[k : k + 1, :], target[k : k + 1, :], by_slot)
    marks[dp] = jnp.full((slots, LANES), -1.0, F32)
    marks[dp, :, 0:n_q] = by_slot
    mark_copies = []
    for d in range(1, n_dp):
        there = {"dp": (dp + d) % n_dp}
        mark_copies.append(
            start(
                remote(marks.at[dp], marks.at[dp], mark_sem.at[0, d], mark_sem.at[1, d], there)
            )
        )
    row_at = lax.broadcasted_iota(jnp.int32, (padded, LANES), 0)
    for p in range(held_count):
        bias_ref[p] = jnp.where(row_at < lengths[p], 0.0, DEAD)
    pair_copies[0].wait_recv()
    embed[...] += pair_recv[0]
    own_load.wait()
    line_prepare(0)
    for k in range(2, lines):
        hop(k)
        line_prepare(k - 1)

    total = embed[...]
    for dx in range(1, chips):
        chip_copies[dx].wait_recv()
        total = total + chip_recv[dx].astype(F32)
    embed[...] = total
    for p in range(held_count):
        piece = embed[p * LP : (p + 1) * LP, :]
        norms = jnp.sqrt(jnp.sum(piece * piece, axis=-1, keepdims=True) + norm_eps)
        units = piece / norms
        unit_ref[p, 0:LP, :] = units
        unit_ref[p, LP:padded, :] = jnp.zeros((padded - LP, DIM), F32)
        norm_ref[p, 0:LP, :] = jnp.broadcast_to(1.0 / norms, (LP, DIM))
        vectors[p] = unit_ref[p].astype(BF16)

    if lines > 1:
        line_prepare(lines - 1)

    def score_line(at, carry):
        score(at * sides + side)
        return carry

    lax.fori_loop(0, lines, score_line, 0)
    for copy in mark_copies:
        copy.wait_recv()
    for v in range(slots):
        s, c = v // cap, v % cap
        marks_by_slot[s, c * n_dp : (c + 1) * n_dp, :] = marks[:, v, :]
    for k in range(lines):
        side_arrives(k)

    spread = (
        lax.broadcasted_iota(jnp.int32, (n_q * LQ, LANES), 0) // LQ
        == lax.broadcasted_iota(jnp.int32, (n_q * LQ, LANES), 1)
    ).astype(BF16)

    def split(value):
        high = value.astype(BF16)
        rest = value - high.astype(F32)
        middle = rest.astype(BF16)
        low = (rest - middle.astype(F32)).astype(BF16)
        return jnp.concatenate([high, middle, low], axis=0)

    def joined(value):
        return value[0:slots] + value[slots : 2 * slots] + value[2 * slots : 3 * slots]

    sums = totals[...]
    own_slots = smooth_tau * joined(
        jnp.dot(split(jnp.log(sums)), spread, preferred_element_type=F32)
    )
    own_marks = marks_by_slot[dp]
    student = jnp.where(own_marks >= 0.0, jnp.exp(own_slots), 0.0)
    mine = student[0:n_dp, :]
    for c in range(1, cap):
        mine = mine + student[c * n_dp : (c + 1) * n_dp, :]
    shares[dp] = mine
    share_copies, score_copies = [], []
    for d in range(1, n_dp):
        there = {"dp": (dp + d) % n_dp}
        share_copies.append(
            start(
                remote(
                    shares.at[dp], shares.at[dp], share_sem.at[0, d], share_sem.at[1, d], there
                )
            )
        )
    slot_scores[dp] = own_slots
    per_sum = loss_scale / sums
    for copy in share_copies:
        copy.wait_recv()

    whole = jnp.sum(shares[...], axis=0)
    whole = jnp.concatenate([whole] * cap, axis=0)
    slot_grad = jnp.where(own_marks >= 0.0, student / whole - own_marks, 0.0)
    scale_ref[...] = (
        joined(
            lax.dot_general(
                split(slot_grad), spread, (((1,), (1,)), ((), ())), preferred_element_type=F32
            )
        )
        * per_sum
    )
    def back(r, carry):
        rows_r = query_vecs[r]
        for c in range(cap):
            pair = r * cap + c
            coefficient = (powered[pair] * scale_ref[pl.ds(c * n_dp + r, 1), :]).astype(BF16)
            backs[pair] = jnp.dot(coefficient, rows_r, preferred_element_type=F32)
        return carry

    lax.fori_loop(0, n_dp, back, 0, unroll=4)

    for d in range(1, n_dp):
        there = {"dp": (dp + d) % n_dp}
        score_copies.append(
            start(
                remote(
                    slot_scores.at[dp],
                    slot_scores.at[dp],
                    score_sem.at[0, d],
                    score_sem.at[1, d],
                    there,
                )
            )
        )

    def weigh(block):
        return lax.dot_general(
            embed_grads[block], held[block], (((0,), (0,)), ((), ())), preferred_element_type=F32
        )

    gchip_copies = [[] for _ in range(chips)]
    gpair_copies = [[] for _ in range(chips)]

    def forward(source, piece, dx):
        begin, size = piece
        cut = embed_grads.at[source, pl.ds(begin, size)]
        at = len(gpair_copies[dx])
        gpair_copies[dx].append(
            start(remote(cut, cut, gpair_sem.at[0, dx, at], gpair_sem.at[1, dx, at], partner))
        )

    pieces = []
    ready, sent_rows = 0, 0
    step = max(8, padded // ADD_CUTS)
    while ready < held_count:
        group = range(ready, min(ready + 2, held_count))
        grown_parts = [[] for _ in group]
        for cut in range(0, padded, step):

            def add(pair, sofar):
                piece = backs[pair, cut : cut + step, :]
                which = selected[pair % cap, pair // cap]
                return tuple(
                    now + jnp.where(which == p, piece, 0.0) for now, p in zip(sofar, group)
                )

            zero = jnp.zeros((step, DIM), F32)
            done = lax.fori_loop(0, slots, add, tuple(zero for _ in group), unroll=ADD_UNROLL)
            for keep, value in zip(grown_parts, done):
                keep.append(value)
        for keep, p in zip(grown_parts, group):
            for at, value in enumerate(keep):
                backs_sum = value
                begin = at * step
                size = min(step, LP - begin)
                units = unit_ref[p, begin : begin + size, :]
                along_unit = jnp.sum(units * backs_sum[0:size], axis=-1, keepdims=True)
                grad_rows[p * LP + begin : p * LP + begin + size, :] = (
                    backs_sum[0:size] - units * along_unit
                ) * norm_ref[p, begin : begin + size, :]
        ready = group[-1] + 1
        until = rows if ready == held_count else ready * LP // 16 * 16
        embed_grads[mp, sent_rows:until, :] = grad_rows[sent_rows:until, :].astype(BF16)
        piece = (sent_rows, until - sent_rows)
        pieces.append(piece)
        sent_rows = until
        cut = embed_grads.at[mp, pl.ds(piece[0], piece[1])]
        at = len(pieces) - 1
        for dx in range(1, chips):
            gchip_copies[dx].append(
                start(
                    remote(
                        cut,
                        cut,
                        gchip_sem.at[0, dx, at],
                        gchip_sem.at[1, dx, at],
                        {"mp": mp_at(dx, core)},
                    )
                )
            )
        forward(mp, piece, 0)

    acc[...] = weigh(mp)
    for copy in gpair_copies[0]:
        copy.wait_recv()
    acc[...] += weigh(mp_at(0, other))
    for dx in range(1, chips):
        source = ((chip - dx + chips) % chips) * 2 + core
        for at, piece in enumerate(pieces):
            gchip_copies[dx][at].wait_recv()
            forward(source, piece, dx)
        acc[...] += weigh(source)
    for dx in range(1, chips):
        for copy in gpair_copies[dx]:
            copy.wait_recv()
        acc[...] += weigh(((chip - dx + chips) % chips) * 2 + other)

    share = part_send.shape[1]
    part_send[...] = jnp.transpose(acc[...]).astype(BF16).reshape(n_dp, share, DIM)
    part_copies = []
    for d in range(1, n_dp):
        to = (dp + d) % n_dp
        part_copies.append(
            start(
                remote(
                    part_send.at[to],
                    part_recv.at[d],
                    part_sem.at[0, d],
                    part_sem.at[1, d],
                    {"dp": to},
                )
            )
        )
    whole = part_send[dp].astype(F32)
    for d in range(1, n_dp):
        part_copies[d - 1].wait_recv()
        whole = whole + part_recv[d].astype(F32)
    final[...] = whole.astype(BF16)
    final_copies = []
    for d in range(1, n_dp):
        final_copies.append(
            start(
                remote(
                    final,
                    grad_out.at[dp],
                    final_sem.at[0, d],
                    final_sem.at[1, d],
                    {"dp": (dp + d) % n_dp},
                )
            )
        )
    own_out = pltpu.make_async_copy(final, grad_out.at[dp], out_sem)
    own_out.start()

    for copy in score_copies:
        copy.wait_recv()
    for v in range(slots):
        s, c = v // cap, v % cap
        own_scores[v : v + 1, :] = slot_scores[s, pl.ds(c * n_dp + dp, 1), :]
    by_slot = own_scores[:, 0:n_q]
    for k in range(chosen.shape[0]):
        picked[k : k + 1, :] = jnp.sum(
            jnp.where(slot_row == chosen[k : k + 1, :], by_slot, 0.0), axis=0, keepdims=True
        )
    scores_write = pltpu.make_async_copy(picked, scores_out, scores_sem)
    scores_write.start()
    for copy in pending:
        copy.wait_send()

    def sent(at, carry):
        source = at * sides + side
        for part in range(PARTS):

            @pl.when((at <= line) & (line < lines - 1))
            def _():
                step_right(source, part).wait_send()

            @pl.when((at >= line) & (line > 0))
            def _():
                step_left(source, part).wait_send()

            if sides == 2:
                step_side(source, part).wait_send()
        return carry

    lax.fori_loop(0, lines, sent, 0)
    own_out.wait()
    scores_write.wait()
    for copy in final_copies:
        copy.wait_recv()


def finish(scores, grad, scores_out, grad_out):
    scores_out[...] = scores[...]
    grad_out[...] = grad[...].astype(F32)


def on_device(sizes, states, proj, queries, lengths, slot_passage, candidates, teacher):
    n_dp, n_mp, held_count, cap, n_q = sizes
    width = states.shape[1]
    rows = held_count * LP
    padded = (LP + 15) // 16 * 16
    pairs = n_dp * cap
    share = width // n_dp
    query_rows = n_q * LQ
    chips = n_mp // 2
    vmem = pl.BlockSpec(memory_space=pltpu.VMEM)
    smem = pl.BlockSpec(memory_space=pltpu.SMEM)
    hbm = pl.BlockSpec(memory_space=pl.ANY)
    scores, grad = pl.pallas_call(
        functools.partial(kernel, sizes),
        out_shape=(
            jax.ShapeDtypeStruct(candidates.shape[::-1], F32),
            jax.ShapeDtypeStruct((n_dp, share, DIM), BF16),
        ),
        in_specs=[smem, smem, hbm, hbm, hbm, vmem, vmem],
        out_specs=(hbm, hbm),
        scratch_shapes=[
            pltpu.VMEM((n_mp, rows, width), BF16),
            pltpu.VMEM((width, DIM), BF16),
            pltpu.VMEM((chips, rows, DIM), F32),
            pltpu.VMEM((chips, rows, DIM), F32),
            pltpu.VMEM((chips, rows, DIM), F32),
            pltpu.VMEM((chips, rows, DIM), BF16),
            pltpu.VMEM((chips, rows, DIM), BF16),
            pltpu.VMEM((rows, DIM), F32),
            pltpu.VMEM((held_count, padded, DIM), F32),
            pltpu.VMEM((held_count, padded, DIM), F32),
            pltpu.VMEM((held_count, padded, LANES), F32),
            pltpu.VMEM((held_count, padded, DIM), BF16),
            pltpu.VMEM((n_dp, query_rows, DIM), BF16),
            pltpu.VMEM((n_dp, query_rows, DIM), BF16),
            pltpu.VMEM((pairs, padded, query_rows), F32),
            pltpu.VMEM((pairs, query_rows), F32),
            pltpu.VMEM((pairs, query_rows), F32),
            pltpu.VMEM((pairs, LANES), F32),
            pltpu.VMEM((n_dp, pairs, LANES), F32),
            pltpu.VMEM((n_dp, pairs, LANES), F32),
            pltpu.VMEM((n_dp, pairs, LANES), F32),
            pltpu.VMEM((n_dp, n_dp, LANES), F32),
            pltpu.VMEM((pairs, padded, DIM), F32),
            pltpu.VMEM((rows, DIM), F32),
            pltpu.VMEM((n_mp, rows, DIM), BF16),
            pltpu.VMEM((DIM, width), F32),
            pltpu.VMEM((n_dp, share, DIM), BF16),
            pltpu.VMEM((n_dp, share, DIM), BF16),
            pltpu.VMEM((share, DIM), BF16),
            pltpu.SemaphoreType.DMA((n_mp,)),
            pltpu.SemaphoreType.DMA,
            pltpu.SemaphoreType.DMA,
            pltpu.SemaphoreType.DMA((n_dp, PARTS)),
            pltpu.SemaphoreType.DMA((2, chips)),
            pltpu.SemaphoreType.DMA((2, chips)),
            pltpu.SemaphoreType.DMA((2, n_dp, PARTS)),
            pltpu.SemaphoreType.DMA((2, n_dp, PARTS)),
            pltpu.SemaphoreType.DMA((2, n_dp)),
            pltpu.SemaphoreType.DMA((2, n_dp)),
            pltpu.SemaphoreType.DMA((2, n_dp)),
            pltpu.SemaphoreType.DMA((2, chips, held_count)),
            pltpu.SemaphoreType.DMA((2, chips, held_count)),
            pltpu.SemaphoreType.DMA((2, n_dp)),
            pltpu.SemaphoreType.DMA((2, n_dp)),
            pltpu.SemaphoreType.DMA,
            pltpu.VMEM(candidates.shape[::-1], F32),
            pltpu.SemaphoreType.DMA,
        ],
        compiler_params=pltpu.CompilerParams(
            collective_id=0, has_side_effects=True, vmem_limit_bytes=62 * 1024 * 1024
        ),
    )(
        lengths,
        slot_passage.reshape(n_dp, cap).T,
        states.reshape(n_mp, rows, width),
        proj,
        queries,
        candidates.T,
        teacher.T,
    )
    scores, grad = pl.pallas_call(
        finish,
        out_shape=(
            jax.ShapeDtypeStruct(scores.shape, F32),
            jax.ShapeDtypeStruct((width, DIM), F32),
        ),
        in_specs=[vmem, vmem],
        out_specs=(vmem, vmem),
    )(scores, grad.reshape(width, DIM))
    return scores.T, grad


def solution(mesh):
    n_dp, n_mp = mesh.shape["dp"], mesh.shape["mp"]

    def whole(states, proj, queries, lengths, slot_passage, candidates, teacher):
        devices = n_dp * n_mp
        sizes = (
            n_dp,
            n_mp,
            lengths.shape[0] // devices,
            slot_passage.shape[3],
            candidates.shape[0] // devices,
        )
        return jax.shard_map(
            functools.partial(on_device, sizes),
            mesh=mesh,
            in_specs=(
                P("dp", "mp"),
                P("mp", None),
                P(("dp", "mp"), None),
                P(("dp", "mp")),
                P("dp", "mp", None, None),
                P(("dp", "mp"), None),
                P(("dp", "mp"), None),
            ),
            out_specs=(P(("dp", "mp"), None), P("mp", None)),
            check_vma=False,
        )(states, proj, queries, lengths, slot_passage, candidates, teacher)

    return whole
```

```python
import functools

import jax
import jax.numpy as jnp
from jax import lax
from jax.experimental import pallas as pl
from jax.experimental.pallas import tpu as pltpu
from jax.sharding import PartitionSpec as P

DIM = 128
LQ = 32
LP = 180
LANES = 128
PARTS = 2
ADD_CUTS = 2
ADD_UNROLL = 4
LOG2E = 1.4426950408889634
DEAD = -1e30

smooth_tau = 0.0625
loss_scale = 1024.0
norm_eps = 1e-06

MESH = pl.DeviceIdType.MESH
HIGHEST = lax.Precision.HIGHEST
F32 = jnp.float32
BF16 = jnp.bfloat16


def remote(src, dst, send, recv, where):
    return pltpu.make_async_remote_copy(
        src_ref=src, dst_ref=dst, send_sem=send, recv_sem=recv, device_id=where, device_id_type=MESH
    )


def kernel(
    sizes,
    lengths,
    selected,
    states,
    proj,
    queries,
    candidates,
    teacher,
    scores_out,
    grad_out,
    held,
    proj_ref,
    pair_send,
    pair_recv,
    chip_part,
    chip_send,
    chip_recv,
    embed,
    unit_ref,
    norm_ref,
    bias_ref,
    vectors,
    raw_queries,
    query_vecs,
    powered,
    totals,
    scale_ref,
    own_scores,
    marks,
    marks_by_slot,
    slot_scores,
    shares,
    backs,
    grad_rows,
    embed_grads,
    acc,
    part_send,
    part_recv,
    final,
    load_sem,
    own_sem,
    proj_sem,
    left_sem,
    pair_sem,
    chip_sem,
    row_sem,
    side_sem,
    mark_sem,
    share_sem,
    score_sem,
    gpair_sem,
    gchip_sem,
    part_sem,
    final_sem,
    out_sem,
    picked,
    scores_sem,
):
    n_dp, n_mp, held_count, cap, n_q = sizes
    chips = n_mp // 2
    sides = 2 if n_dp % 2 == 0 else 1
    lines = n_dp // sides
    rows = held_count * LP
    padded = vectors.shape[1]
    slots = n_dp * cap
    dp = lax.axis_index("dp")
    mp = lax.axis_index("mp")
    chip, core = mp // 2, mp % 2
    other = 1 - core
    line, side = dp // sides, dp % sides

    barrier = pltpu.get_barrier_semaphore()
    for d in range(1, n_dp):
        pl.semaphore_signal(
            barrier, inc=1, device_id={"dp": (dp + d) % n_dp}, device_id_type=MESH
        )
    for d in range(1, n_mp):
        pl.semaphore_signal(
            barrier, inc=1, device_id={"mp": (mp + d) % n_mp}, device_id_type=MESH
        )

    def mp_at(dx, which):
        return ((chip + dx) % chips) * 2 + which

    proj_load = pltpu.make_async_copy(proj, proj_ref, proj_sem)
    proj_load.start()
    order = []
    for dx in range(1, chips):
        order += [mp_at(dx, other), mp_at(dx, core)]
    order += [mp_at(0, other), mp_at(0, core)]
    loads = []
    for at, block in enumerate(order):
        copy = pltpu.make_async_copy(states.at[block], held.at[block], load_sem.at[at])
        copy.start()
        loads.append(copy)
    own_load = pltpu.make_async_copy(queries, raw_queries.at[dp], own_sem)
    own_load.start()

    pending = []

    def start(copy):
        copy.start()
        pending.append(copy)
        return copy

    half = queries.shape[0] // PARTS

    def rows_of(part):
        return pl.ds(part * half, half)

    def step_right(source, part, own=False):
        there = raw_queries.at[source, rows_of(part)]
        return remote(
            queries.at[rows_of(part)] if own else there,
            there,
            row_sem.at[0, source, part],
            row_sem.at[1, source, part],
            {"dp": jnp.minimum(line + 1, lines - 1) * sides + side},
        )

    def step_left(source, part, own=False):
        there = raw_queries.at[source, rows_of(part)]
        return remote(
            queries.at[rows_of(part)] if own else there,
            there,
            left_sem.at[source, part],
            row_sem.at[1, source, part],
            {"dp": jnp.maximum(line - 1, 0) * sides + side},
        )

    def step_side(source, part, own=False):
        there = raw_queries.at[source, rows_of(part)]
        return remote(
            queries.at[rows_of(part)] if own else there,
            there,
            side_sem.at[0, source, part],
            side_sem.at[1, source, part],
            {"dp": line * sides + (1 - side)},
        )

    pl.semaphore_wait(barrier, n_dp + n_mp - 2)
    for part in range(PARTS):

        @pl.when(line < lines - 1)
        def _():
            step_right(dp, part, True).start()

        @pl.when(line > 0)
        def _():
            step_left(dp, part, True).start()

        if sides == 2:
            step_side(dp, part, True).start()

    partner = {"mp": mp_at(0, other)}
    pair_copies, chip_copies = {}, {}

    def send_pair(dx):
        pair_copies[dx] = start(
            remote(
                pair_send.at[dx],
                pair_recv.at[dx],
                pair_sem.at[0, dx],
                pair_sem.at[1, dx],
                partner,
            )
        )

    def partial(at):
        loads[at].wait()
        return jnp.dot(held[order[at]], proj_ref[...], preferred_element_type=F32)

    def hop(k, parts):
        for part in parts:

            @pl.when(line >= k)
            def _():
                source = (line - k) * sides + side
                copy = step_right(source, part)
                copy.wait_recv()

                @pl.when(line < lines - 1)
                def _():
                    copy.start()

                if sides == 2:
                    step_side(source, part).start()

            @pl.when(line + k < lines)
            def _():
                source = (line + k) * sides + side
                copy = step_left(source, part)
                copy.wait_recv()

                @pl.when(line > 0)
                def _():
                    copy.start()

                if sides == 2:
                    step_side(source, part).start()

    def prepare(r):
        values = raw_queries[r].astype(F32)
        query_vecs[r] = (
            values / jnp.sqrt(jnp.sum(values * values, axis=-1, keepdims=True) + norm_eps)
        ).astype(BF16)

    def score(r):
        rows_r = query_vecs[r]
        for c in range(cap):
            pair = r * cap + c
            p = selected[c, r]
            similar = lax.dot_general(
                vectors[p], rows_r, (((1,), (1,)), ((), ())), preferred_element_type=F32
            )
            dead = jnp.concatenate([bias_ref[p]] * (similar.shape[1] // LANES), axis=1)
            grown = jnp.exp2(similar * (LOG2E / smooth_tau) + dead)
            powered[pair] = grown
            totals[pl.ds(c * n_dp + r, 1), :] = jnp.sum(grown, axis=0, keepdims=True)

    def along_line(k, body):
        def one(j, carry):
            at = line - k + 2 * k * j

            @pl.when((at >= 0) & (at < lines))
            def _():
                body(at)

            return carry

        lax.fori_loop(0, 1 if k == 0 else 2, one, 0)

    def line_prepare(k):
        along_line(k, lambda at: prepare(at * sides + side))

    def side_arrives(k):
        def body(at):
            source = at * sides + 1 - side
            for part in range(PARTS):
                step_side(source, part).wait_recv()
            prepare(source)
            score(source)

        if sides == 2:
            along_line(k, body)

    proj_load.wait()
    for dx in range(1, chips):
        pair_send[dx] = partial(2 * dx - 2)
        send_pair(dx)
        chip_part[dx] = partial(2 * dx - 1)
    for dx in range(1, chips):
        pair_copies[dx].wait_recv()
        chip_send[dx] = (chip_part[dx] + pair_recv[dx]).astype(BF16)
        chip_copies[dx] = start(
            remote(
                chip_send.at[dx],
                chip_recv.at[dx],
                chip_sem.at[0, dx],
                chip_sem.at[1, dx],
                {"mp": mp_at(dx, core)},
            )
        )
    hop(1, (0,))
    pair_send[0] = partial(n_mp - 2)
    send_pair(0)
    hop(1, (1,))
    embed[...] = partial(n_mp - 1)


    target = jnp.exp(teacher[...])
    target = target / jnp.sum(target, axis=0, keepdims=True)
    chosen = candidates[...]
    slot_row = lax.broadcasted_iota(jnp.int32, (slots, n_q), 0)
    by_slot = jnp.full((slots, n_q), -1.0, F32)
    for k in range(chosen.shape[0]):
        by_slot = jnp.where(slot_row == chosen[k : k + 1, :], target[k : k + 1, :], by_slot)
    marks[dp] = jnp.full((slots, LANES), -1.0, F32)
    marks[dp, :, 0:n_q] = by_slot
    row_at = lax.broadcasted_iota(jnp.int32, (padded, LANES), 0)
    for p in range(held_count):
        bias_ref[p] = jnp.where(row_at < lengths[p], 0.0, DEAD)
    own_load.wait()
    line_prepare(0)
    hop(2, (0,))
    hop(2, (1,))
    pair_copies[0].wait_recv()
    embed[...] += pair_recv[0]
    mark_copies = []
    for d in range(1, n_dp):
        there = {"dp": (dp + d) % n_dp}
        mark_copies.append(
            start(
                remote(marks.at[dp], marks.at[dp], mark_sem.at[0, d], mark_sem.at[1, d], there)
            )
        )
    line_prepare(1)
    for k in range(3, lines):
        hop(k, range(PARTS))
        line_prepare(k - 1)

    total = embed[...]
    for dx in range(1, chips):
        chip_copies[dx].wait_recv()
        total = total + chip_recv[dx].astype(F32)
    embed[...] = total
    for p in range(held_count):
        piece = embed[p * LP : (p + 1) * LP, :]
        norms = jnp.sqrt(jnp.sum(piece * piece, axis=-1, keepdims=True) + norm_eps)
        units = piece / norms
        unit_ref[p, 0:LP, :] = units
        unit_ref[p, LP:padded, :] = jnp.zeros((padded - LP, DIM), F32)
        norm_ref[p, 0:LP, :] = jnp.broadcast_to(1.0 / norms, (LP, DIM))
        vectors[p] = unit_ref[p].astype(BF16)

    if lines > 1:
        line_prepare(lines - 1)

    def score_line(at, carry):
        score(at * sides + side)
        return carry

    lax.fori_loop(0, lines, score_line, 0)
    for copy in mark_copies:
        copy.wait_recv()
    for v in range(slots):
        s, c = v // cap, v % cap
        marks_by_slot[s, c * n_dp : (c + 1) * n_dp, :] = marks[:, v, :]
    for k in range(lines):
        side_arrives(k)

    spread = (
        lax.broadcasted_iota(jnp.int32, (n_q * LQ, LANES), 0) // LQ
        == lax.broadcasted_iota(jnp.int32, (n_q * LQ, LANES), 1)
    ).astype(BF16)

    def split(value):
        high = value.astype(BF16)
        rest = value - high.astype(F32)
        middle = rest.astype(BF16)
        low = (rest - middle.astype(F32)).astype(BF16)
        return jnp.concatenate([high, middle, low], axis=0)

    def joined(value):
        return value[0:slots] + value[slots : 2 * slots] + value[2 * slots : 3 * slots]

    sums = totals[...]
    own_slots = smooth_tau * joined(
        jnp.dot(split(jnp.log(sums)), spread, preferred_element_type=F32)
    )
    own_marks = marks_by_slot[dp]
    student = jnp.where(own_marks >= 0.0, jnp.exp(own_slots), 0.0)
    mine = student[0:n_dp, :]
    for c in range(1, cap):
        mine = mine + student[c * n_dp : (c + 1) * n_dp, :]
    shares[dp] = mine
    share_copies, score_copies = [], []
    for d in range(1, n_dp):
        there = {"dp": (dp + d) % n_dp}
        share_copies.append(
            start(
                remote(
                    shares.at[dp], shares.at[dp], share_sem.at[0, d], share_sem.at[1, d], there
                )
            )
        )
    slot_scores[dp] = own_slots
    per_sum = loss_scale / sums
    for copy in share_copies:
        copy.wait_recv()

    whole = jnp.sum(shares[...], axis=0)
    whole = jnp.concatenate([whole] * cap, axis=0)
    slot_grad = jnp.where(own_marks >= 0.0, student / whole - own_marks, 0.0)
    scale_ref[...] = (
        joined(
            lax.dot_general(
                split(slot_grad), spread, (((1,), (1,)), ((), ())), preferred_element_type=F32
            )
        )
        * per_sum
    )
    def back(r, carry):
        rows_r = query_vecs[r]
        for c in range(cap):
            pair = r * cap + c
            coefficient = (powered[pair] * scale_ref[pl.ds(c * n_dp + r, 1), :]).astype(BF16)
            backs[pair] = jnp.dot(coefficient, rows_r, preferred_element_type=F32)
        return carry

    lax.fori_loop(0, n_dp, back, 0, unroll=4)

    for d in range(1, n_dp):
        there = {"dp": (dp + d) % n_dp}
        score_copies.append(
            start(
                remote(
                    slot_scores.at[dp],
                    slot_scores.at[dp],
                    score_sem.at[0, d],
                    score_sem.at[1, d],
                    there,
                )
            )
        )

    def weigh(block):
        return lax.dot_general(
            embed_grads[block], held[block], (((0,), (0,)), ((), ())), preferred_element_type=F32
        )

    gchip_copies = [[] for _ in range(chips)]
    gpair_copies = [[] for _ in range(chips)]

    def forward(source, piece, dx):
        begin, size = piece
        cut = embed_grads.at[source, pl.ds(begin, size)]
        at = len(gpair_copies[dx])
        gpair_copies[dx].append(
            start(remote(cut, cut, gpair_sem.at[0, dx, at], gpair_sem.at[1, dx, at], partner))
        )

    pieces = []
    ready, sent_rows = 0, 0
    step = max(8, padded // ADD_CUTS)
    while ready < held_count:
        group = range(ready, min(ready + 2, held_count))
        grown_parts = [[] for _ in group]
        for cut in range(0, padded, step):

            def add(pair, sofar):
                piece = backs[pair, cut : cut + step, :]
                which = selected[pair % cap, pair // cap]
                return tuple(
                    now + jnp.where(which == p, piece, 0.0) for now, p in zip(sofar, group)
                )

            zero = jnp.zeros((step, DIM), F32)
            done = lax.fori_loop(0, slots, add, tuple(zero for _ in group), unroll=ADD_UNROLL)
            for keep, value in zip(grown_parts, done):
                keep.append(value)
        for keep, p in zip(grown_parts, group):
            for at, value in enumerate(keep):
                backs_sum = value
                begin = at * step
                size = min(step, LP - begin)
                units = unit_ref[p, begin : begin + size, :]
                along_unit = jnp.sum(units * backs_sum[0:size], axis=-1, keepdims=True)
                grad_rows[p * LP + begin : p * LP + begin + size, :] = (
                    backs_sum[0:size] - units * along_unit
                ) * norm_ref[p, begin : begin + size, :]
        ready = group[-1] + 1
        until = rows if ready == held_count else ready * LP // 16 * 16
        embed_grads[mp, sent_rows:until, :] = grad_rows[sent_rows:until, :].astype(BF16)
        piece = (sent_rows, until - sent_rows)
        pieces.append(piece)
        sent_rows = until
        cut = embed_grads.at[mp, pl.ds(piece[0], piece[1])]
        at = len(pieces) - 1
        for dx in range(1, chips):
            gchip_copies[dx].append(
                start(
                    remote(
                        cut,
                        cut,
                        gchip_sem.at[0, dx, at],
                        gchip_sem.at[1, dx, at],
                        {"mp": mp_at(dx, core)},
                    )
                )
            )
        forward(mp, piece, 0)

    acc[...] = weigh(mp)
    for copy in gpair_copies[0]:
        copy.wait_recv()
    acc[...] += weigh(mp_at(0, other))
    for dx in range(1, chips):
        source = ((chip - dx + chips) % chips) * 2 + core
        for at, piece in enumerate(pieces):
            gchip_copies[dx][at].wait_recv()
            forward(source, piece, dx)
        acc[...] += weigh(source)
    for dx in range(1, chips):
        for copy in gpair_copies[dx]:
            copy.wait_recv()
        acc[...] += weigh(((chip - dx + chips) % chips) * 2 + other)

    share = part_send.shape[1]
    part_send[...] = jnp.transpose(acc[...]).astype(BF16).reshape(n_dp, share, DIM)
    part_copies = []
    for d in range(1, n_dp):
        to = (dp + d) % n_dp
        part_copies.append(
            start(
                remote(
                    part_send.at[to],
                    part_recv.at[d],
                    part_sem.at[0, d],
                    part_sem.at[1, d],
                    {"dp": to},
                )
            )
        )
    whole = part_send[dp].astype(F32)
    for d in range(1, n_dp):
        part_copies[d - 1].wait_recv()
        whole = whole + part_recv[d].astype(F32)
    final[...] = whole.astype(BF16)
    final_copies = []
    for d in range(1, n_dp):
        final_copies.append(
            start(
                remote(
                    final,
                    grad_out.at[dp],
                    final_sem.at[0, d],
                    final_sem.at[1, d],
                    {"dp": (dp + d) % n_dp},
                )
            )
        )
    own_out = pltpu.make_async_copy(final, grad_out.at[dp], out_sem)
    own_out.start()

    for copy in score_copies:
        copy.wait_recv()
    for v in range(slots):
        s, c = v // cap, v % cap
        own_scores[v : v + 1, :] = slot_scores[s, pl.ds(c * n_dp + dp, 1), :]
    by_slot = own_scores[:, 0:n_q]
    for k in range(chosen.shape[0]):
        picked[k : k + 1, :] = jnp.sum(
            jnp.where(slot_row == chosen[k : k + 1, :], by_slot, 0.0), axis=0, keepdims=True
        )
    scores_write = pltpu.make_async_copy(picked, scores_out, scores_sem)
    scores_write.start()
    for copy in pending:
        copy.wait_send()

    def sent(at, carry):
        source = at * sides + side
        for part in range(PARTS):

            @pl.when((at <= line) & (line < lines - 1))
            def _():
                step_right(source, part).wait_send()

            @pl.when((at >= line) & (line > 0))
            def _():
                step_left(source, part).wait_send()

            if sides == 2:
                step_side(source, part).wait_send()
        return carry

    lax.fori_loop(0, lines, sent, 0)
    own_out.wait()
    scores_write.wait()
    for copy in final_copies:
        copy.wait_recv()


def finish(scores, grad, scores_out, grad_out):
    scores_out[...] = scores[...]
    grad_out[...] = grad[...].astype(F32)


def on_device(sizes, states, proj, queries, lengths, slot_passage, candidates, teacher):
    n_dp, n_mp, held_count, cap, n_q = sizes
    width = states.shape[1]
    rows = held_count * LP
    padded = (LP + 15) // 16 * 16
    pairs = n_dp * cap
    share = width // n_dp
    query_rows = n_q * LQ
    chips = n_mp // 2
    vmem = pl.BlockSpec(memory_space=pltpu.VMEM)
    smem = pl.BlockSpec(memory_space=pltpu.SMEM)
    hbm = pl.BlockSpec(memory_space=pl.ANY)
    scores, grad = pl.pallas_call(
        functools.partial(kernel, sizes),
        out_shape=(
            jax.ShapeDtypeStruct(candidates.shape[::-1], F32),
            jax.ShapeDtypeStruct((n_dp, share, DIM), BF16),
        ),
        in_specs=[smem, smem, hbm, hbm, hbm, vmem, vmem],
        out_specs=(hbm, hbm),
        scratch_shapes=[
            pltpu.VMEM((n_mp, rows, width), BF16),
            pltpu.VMEM((width, DIM), BF16),
            pltpu.VMEM((chips, rows, DIM), F32),
            pltpu.VMEM((chips, rows, DIM), F32),
            pltpu.VMEM((chips, rows, DIM), F32),
            pltpu.VMEM((chips, rows, DIM), BF16),
            pltpu.VMEM((chips, rows, DIM), BF16),
            pltpu.VMEM((rows, DIM), F32),
            pltpu.VMEM((held_count, padded, DIM), F32),
            pltpu.VMEM((held_count, padded, DIM), F32),
            pltpu.VMEM((held_count, padded, LANES), F32),
            pltpu.VMEM((held_count, padded, DIM), BF16),
            pltpu.VMEM((n_dp, query_rows, DIM), BF16),
            pltpu.VMEM((n_dp, query_rows, DIM), BF16),
            pltpu.VMEM((pairs, padded, query_rows), F32),
            pltpu.VMEM((pairs, query_rows), F32),
            pltpu.VMEM((pairs, query_rows), F32),
            pltpu.VMEM((pairs, LANES), F32),
            pltpu.VMEM((n_dp, pairs, LANES), F32),
            pltpu.VMEM((n_dp, pairs, LANES), F32),
            pltpu.VMEM((n_dp, pairs, LANES), F32),
            pltpu.VMEM((n_dp, n_dp, LANES), F32),
            pltpu.VMEM((pairs, padded, DIM), F32),
            pltpu.VMEM((rows, DIM), F32),
            pltpu.VMEM((n_mp, rows, DIM), BF16),
            pltpu.VMEM((DIM, width), F32),
            pltpu.VMEM((n_dp, share, DIM), BF16),
            pltpu.VMEM((n_dp, share, DIM), BF16),
            pltpu.VMEM((share, DIM), BF16),
            pltpu.SemaphoreType.DMA((n_mp,)),
            pltpu.SemaphoreType.DMA,
            pltpu.SemaphoreType.DMA,
            pltpu.SemaphoreType.DMA((n_dp, PARTS)),
            pltpu.SemaphoreType.DMA((2, chips)),
            pltpu.SemaphoreType.DMA((2, chips)),
            pltpu.SemaphoreType.DMA((2, n_dp, PARTS)),
            pltpu.SemaphoreType.DMA((2, n_dp, PARTS)),
            pltpu.SemaphoreType.DMA((2, n_dp)),
            pltpu.SemaphoreType.DMA((2, n_dp)),
            pltpu.SemaphoreType.DMA((2, n_dp)),
            pltpu.SemaphoreType.DMA((2, chips, held_count)),
            pltpu.SemaphoreType.DMA((2, chips, held_count)),
            pltpu.SemaphoreType.DMA((2, n_dp)),
            pltpu.SemaphoreType.DMA((2, n_dp)),
            pltpu.SemaphoreType.DMA,
            pltpu.VMEM(candidates.shape[::-1], F32),
            pltpu.SemaphoreType.DMA,
        ],
        compiler_params=pltpu.CompilerParams(
            collective_id=0, has_side_effects=True, vmem_limit_bytes=62 * 1024 * 1024
        ),
    )(
        lengths,
        slot_passage.reshape(n_dp, cap).T,
        states.reshape(n_mp, rows, width),
        proj,
        queries,
        candidates.T,
        teacher.T,
    )
    scores, grad = pl.pallas_call(
        finish,
        out_shape=(
            jax.ShapeDtypeStruct(scores.shape, F32),
            jax.ShapeDtypeStruct((width, DIM), F32),
        ),
        in_specs=[vmem, vmem],
        out_specs=(vmem, vmem),
    )(scores, grad.reshape(width, DIM))
    return scores.T, grad


def solution(mesh):
    n_dp, n_mp = mesh.shape["dp"], mesh.shape["mp"]

    def whole(states, proj, queries, lengths, slot_passage, candidates, teacher):
        devices = n_dp * n_mp
        sizes = (
            n_dp,
            n_mp,
            lengths.shape[0] // devices,
            slot_passage.shape[3],
            candidates.shape[0] // devices,
        )
        return jax.shard_map(
            functools.partial(on_device, sizes),
            mesh=mesh,
            in_specs=(
                P("dp", "mp"),
                P("mp", None),
                P(("dp", "mp"), None),
                P(("dp", "mp")),
                P("dp", "mp", None, None),
                P(("dp", "mp"), None),
                P(("dp", "mp"), None),
            ),
            out_specs=(P(("dp", "mp"), None), P("mp", None)),
            check_vma=False,
        )(states, proj, queries, lengths, slot_passage, candidates, teacher)

    return whole
```

```python
import functools

import jax
import jax.numpy as jnp
from jax import lax
from jax.experimental import pallas as pl
from jax.experimental.pallas import tpu as pltpu
from jax.sharding import PartitionSpec as P

DIM = 128
LQ = 32
LP = 180
LANES = 128
PARTS = 2
ADD_CUTS = 2
ADD_UNROLL = 4
LOG2E = 1.4426950408889634
DEAD = -1e30

smooth_tau = 0.0625
loss_scale = 1024.0
norm_eps = 1e-06

MESH = pl.DeviceIdType.MESH
HIGHEST = lax.Precision.HIGHEST
F32 = jnp.float32
BF16 = jnp.bfloat16


def remote(src, dst, send, recv, where):
    return pltpu.make_async_remote_copy(
        src_ref=src, dst_ref=dst, send_sem=send, recv_sem=recv, device_id=where, device_id_type=MESH
    )


def kernel(
    sizes,
    lengths,
    selected,
    states,
    proj,
    queries,
    candidates,
    teacher,
    scores_out,
    grad_out,
    held,
    proj_ref,
    pair_send,
    pair_recv,
    chip_part,
    chip_send,
    chip_recv,
    embed,
    unit_ref,
    norm_ref,
    bias_ref,
    vectors,
    raw_queries,
    query_vecs,
    powered,
    totals,
    scale_ref,
    own_scores,
    marks,
    marks_by_slot,
    slot_scores,
    shares,
    backs,
    grad_rows,
    embed_grads,
    acc,
    part_send,
    part_recv,
    final,
    load_sem,
    own_sem,
    proj_sem,
    left_sem,
    pair_sem,
    chip_sem,
    row_sem,
    side_sem,
    mark_sem,
    share_sem,
    score_sem,
    gpair_sem,
    gchip_sem,
    part_sem,
    final_sem,
    out_sem,
    picked,
    scores_sem,
):
    n_dp, n_mp, held_count, cap, n_q = sizes
    chips = n_mp // 2
    sides = 2 if n_dp % 2 == 0 else 1
    lines = n_dp // sides
    rows = held_count * LP
    padded = vectors.shape[1]
    slots = n_dp * cap
    dp = lax.axis_index("dp")
    mp = lax.axis_index("mp")
    chip, core = mp // 2, mp % 2
    other = 1 - core
    line, side = dp // sides, dp % sides

    barrier = pltpu.get_barrier_semaphore()
    for d in range(1, n_dp):
        pl.semaphore_signal(
            barrier, inc=1, device_id={"dp": (dp + d) % n_dp}, device_id_type=MESH
        )
    for d in range(1, n_mp):
        pl.semaphore_signal(
            barrier, inc=1, device_id={"mp": (mp + d) % n_mp}, device_id_type=MESH
        )

    def mp_at(dx, which):
        return ((chip + dx) % chips) * 2 + which

    proj_load = pltpu.make_async_copy(proj, proj_ref, proj_sem)
    proj_load.start()
    order = []
    for dx in range(1, chips):
        order += [mp_at(dx, other), mp_at(dx, core)]
    order += [mp_at(0, other), mp_at(0, core)]
    loads = []
    for at, block in enumerate(order):
        copy = pltpu.make_async_copy(states.at[block], held.at[block], load_sem.at[at])
        copy.start()
        loads.append(copy)
    own_load = pltpu.make_async_copy(queries, raw_queries.at[dp], own_sem)
    own_load.start()

    pending = []

    def start(copy):
        copy.start()
        pending.append(copy)
        return copy

    half = queries.shape[0] // PARTS

    def rows_of(part):
        return pl.ds(part * half, half)

    def step_right(source, part, own=False):
        there = raw_queries.at[source, rows_of(part)]
        return remote(
            queries.at[rows_of(part)] if own else there,
            there,
            row_sem.at[0, source, part],
            row_sem.at[1, source, part],
            {"dp": jnp.minimum(line + 1, lines - 1) * sides + side},
        )

    def step_left(source, part, own=False):
        there = raw_queries.at[source, rows_of(part)]
        return remote(
            queries.at[rows_of(part)] if own else there,
            there,
            left_sem.at[source, part],
            row_sem.at[1, source, part],
            {"dp": jnp.maximum(line - 1, 0) * sides + side},
        )

    def step_side(source, part, own=False):
        there = raw_queries.at[source, rows_of(part)]
        return remote(
            queries.at[rows_of(part)] if own else there,
            there,
            side_sem.at[0, source, part],
            side_sem.at[1, source, part],
            {"dp": line * sides + (1 - side)},
        )

    pl.semaphore_wait(barrier, n_dp + n_mp - 2)
    for part in range(PARTS):

        @pl.when(line < lines - 1)
        def _():
            step_right(dp, part, True).start()

        @pl.when(line > 0)
        def _():
            step_left(dp, part, True).start()

    for part in range(PARTS):
        if sides == 2:
            step_side(dp, part, True).start()

    partner = {"mp": mp_at(0, other)}
    pair_copies, chip_copies = {}, {}

    def send_pair(dx):
        pair_copies[dx] = start(
            remote(
                pair_send.at[dx],
                pair_recv.at[dx],
                pair_sem.at[0, dx],
                pair_sem.at[1, dx],
                partner,
            )
        )

    def partial(at):
        loads[at].wait()
        return jnp.dot(held[order[at]], proj_ref[...], preferred_element_type=F32)

    def hop(k, parts):
        for part in parts:

            @pl.when(line >= k)
            def _():
                source = (line - k) * sides + side
                copy = step_right(source, part)
                copy.wait_recv()

                @pl.when(line < lines - 1)
                def _():
                    copy.start()

                if sides == 2:
                    step_side(source, part).start()

            @pl.when(line + k < lines)
            def _():
                source = (line + k) * sides + side
                copy = step_left(source, part)
                copy.wait_recv()

                @pl.when(line > 0)
                def _():
                    copy.start()

                if sides == 2:
                    step_side(source, part).start()

    def prepare(r):
        values = raw_queries[r].astype(F32)
        query_vecs[r] = (
            values / jnp.sqrt(jnp.sum(values * values, axis=-1, keepdims=True) + norm_eps)
        ).astype(BF16)

    def score(r):
        rows_r = query_vecs[r]
        for c in range(cap):
            pair = r * cap + c
            p = selected[c, r]
            similar = lax.dot_general(
                vectors[p], rows_r, (((1,), (1,)), ((), ())), preferred_element_type=F32
            )
            dead = jnp.concatenate([bias_ref[p]] * (similar.shape[1] // LANES), axis=1)
            grown = jnp.exp2(similar * (LOG2E / smooth_tau) + dead)
            powered[pair] = grown
            totals[pl.ds(c * n_dp + r, 1), :] = jnp.sum(grown, axis=0, keepdims=True)

    def along_line(k, body):
        def one(j, carry):
            at = line - k + 2 * k * j

            @pl.when((at >= 0) & (at < lines))
            def _():
                body(at)

            return carry

        lax.fori_loop(0, 1 if k == 0 else 2, one, 0)

    def line_prepare(k):
        along_line(k, lambda at: prepare(at * sides + side))

    def side_arrives(k):
        def body(at):
            source = at * sides + 1 - side
            for part in range(PARTS):
                step_side(source, part).wait_recv()
            prepare(source)
            score(source)

        if sides == 2:
            along_line(k, body)

    proj_load.wait()
    for dx in range(1, chips):
        pair_send[dx] = partial(2 * dx - 2)
        send_pair(dx)
        chip_part[dx] = partial(2 * dx - 1)
    for dx in range(1, chips):
        pair_copies[dx].wait_recv()
        chip_send[dx] = (chip_part[dx] + pair_recv[dx]).astype(BF16)
        chip_copies[dx] = start(
            remote(
                chip_send.at[dx],
                chip_recv.at[dx],
                chip_sem.at[0, dx],
                chip_sem.at[1, dx],
                {"mp": mp_at(dx, core)},
            )
        )
    hop(1, (0,))
    pair_send[0] = partial(n_mp - 2)
    send_pair(0)
    hop(1, (1,))
    embed[...] = partial(n_mp - 1)


    target = jnp.exp(teacher[...])
    target = target / jnp.sum(target, axis=0, keepdims=True)
    chosen = candidates[...]
    slot_row = lax.broadcasted_iota(jnp.int32, (slots, n_q), 0)
    by_slot = jnp.full((slots, n_q), -1.0, F32)
    for k in range(chosen.shape[0]):
        by_slot = jnp.where(slot_row == chosen[k : k + 1, :], target[k : k + 1, :], by_slot)
    marks[dp] = jnp.full((slots, LANES), -1.0, F32)
    marks[dp, :, 0:n_q] = by_slot
    row_at = lax.broadcasted_iota(jnp.int32, (padded, LANES), 0)
    for p in range(held_count):
        bias_ref[p] = jnp.where(row_at < lengths[p], 0.0, DEAD)
    own_load.wait()
    line_prepare(0)
    hop(2, (0,))
    hop(2, (1,))
    pair_copies[0].wait_recv()
    embed[...] += pair_recv[0]
    mark_copies = []
    for d in range(1, n_dp):
        there = {"dp": (dp + d) % n_dp}
        mark_copies.append(
            start(
                remote(marks.at[dp], marks.at[dp], mark_sem.at[0, d], mark_sem.at[1, d], there)
            )
        )
    line_prepare(1)
    for k in range(3, lines - 1):
        hop(k, range(PARTS))
        line_prepare(k - 1)
    total = embed[...]
    for dx in range(1, chips):
        chip_copies[dx].wait_recv()
        total = total + chip_recv[dx].astype(F32)
    embed[...] = total
    for p in range(held_count):
        piece = embed[p * LP : (p + 1) * LP, :]
        norms = jnp.sqrt(jnp.sum(piece * piece, axis=-1, keepdims=True) + norm_eps)
        units = piece / norms
        unit_ref[p, 0:LP, :] = units
        unit_ref[p, LP:padded, :] = jnp.zeros((padded - LP, DIM), F32)
        norm_ref[p, 0:LP, :] = jnp.broadcast_to(1.0 / norms, (LP, DIM))
        vectors[p] = unit_ref[p].astype(BF16)

    def line_score(k):
        along_line(k, lambda at: score(at * sides + side))

    early = max(lines - 2, 0)
    for k in range(early):
        line_score(k)
    if lines > 3:
        hop(lines - 1, range(PARTS))
        line_prepare(lines - 2)
    side_arrives(0)
    if lines > 2:
        line_score(lines - 2)
    if lines > 1:
        line_prepare(lines - 1)
    if early < lines - 1 or lines == 1:
        line_score(lines - 1)
    for copy in mark_copies:
        copy.wait_recv()
    for v in range(slots):
        s, c = v // cap, v % cap
        marks_by_slot[s, c * n_dp : (c + 1) * n_dp, :] = marks[:, v, :]
    for k in range(1, lines):
        side_arrives(k)

    spread = (
        lax.broadcasted_iota(jnp.int32, (n_q * LQ, LANES), 0) // LQ
        == lax.broadcasted_iota(jnp.int32, (n_q * LQ, LANES), 1)
    ).astype(BF16)

    def split(value):
        high = value.astype(BF16)
        rest = value - high.astype(F32)
        middle = rest.astype(BF16)
        low = (rest - middle.astype(F32)).astype(BF16)
        return jnp.concatenate([high, middle, low], axis=0)

    def joined(value):
        return value[0:slots] + value[slots : 2 * slots] + value[2 * slots : 3 * slots]

    sums = totals[...]
    own_slots = smooth_tau * joined(
        jnp.dot(split(jnp.log(sums)), spread, preferred_element_type=F32)
    )
    own_marks = marks_by_slot[dp]
    student = jnp.where(own_marks >= 0.0, jnp.exp(own_slots), 0.0)
    mine = student[0:n_dp, :]
    for c in range(1, cap):
        mine = mine + student[c * n_dp : (c + 1) * n_dp, :]
    shares[dp] = mine
    share_copies, score_copies = [], []
    for d in range(1, n_dp):
        there = {"dp": (dp + d) % n_dp}
        share_copies.append(
            start(
                remote(
                    shares.at[dp], shares.at[dp], share_sem.at[0, d], share_sem.at[1, d], there
                )
            )
        )
    slot_scores[dp] = own_slots
    per_sum = loss_scale / sums
    for copy in share_copies:
        copy.wait_recv()

    whole = jnp.sum(shares[...], axis=0)
    whole = jnp.concatenate([whole] * cap, axis=0)
    slot_grad = jnp.where(own_marks >= 0.0, student / whole - own_marks, 0.0)
    scale_ref[...] = (
        joined(
            lax.dot_general(
                split(slot_grad), spread, (((1,), (1,)), ((), ())), preferred_element_type=F32
            )
        )
        * per_sum
    )
    def back(r, carry):
        rows_r = query_vecs[r]
        for c in range(cap):
            pair = r * cap + c
            coefficient = (powered[pair] * scale_ref[pl.ds(c * n_dp + r, 1), :]).astype(BF16)
            backs[pair] = jnp.dot(coefficient, rows_r, preferred_element_type=F32)
        return carry

    lax.fori_loop(0, n_dp, back, 0, unroll=8)

    for d in range(1, n_dp):
        there = {"dp": (dp + d) % n_dp}
        score_copies.append(
            start(
                remote(
                    slot_scores.at[dp],
                    slot_scores.at[dp],
                    score_sem.at[0, d],
                    score_sem.at[1, d],
                    there,
                )
            )
        )

    def weigh(block):
        return lax.dot_general(
            embed_grads[block], held[block], (((0,), (0,)), ((), ())), preferred_element_type=F32
        )

    gchip_copies = [[] for _ in range(chips)]
    gpair_copies = [[] for _ in range(chips)]

    def forward(source, piece, dx):
        begin, size = piece
        cut = embed_grads.at[source, pl.ds(begin, size)]
        at = len(gpair_copies[dx])
        gpair_copies[dx].append(
            start(remote(cut, cut, gpair_sem.at[0, dx, at], gpair_sem.at[1, dx, at], partner))
        )

    pieces = []
    ready, sent_rows = 0, 0
    step = max(8, padded // ADD_CUTS)
    while ready < held_count:
        group = range(ready, min(ready + 2, held_count))
        grown_parts = [[] for _ in group]
        for cut in range(0, padded, step):

            def add(pair, sofar):
                piece = backs[pair, cut : cut + step, :]
                which = selected[pair % cap, pair // cap]
                return tuple(
                    now + jnp.where(which == p, piece, 0.0) for now, p in zip(sofar, group)
                )

            zero = jnp.zeros((step, DIM), F32)
            done = lax.fori_loop(0, slots, add, tuple(zero for _ in group), unroll=ADD_UNROLL)
            for keep, value in zip(grown_parts, done):
                keep.append(value)
        for keep, p in zip(grown_parts, group):
            for at, value in enumerate(keep):
                backs_sum = value
                begin = at * step
                size = min(step, LP - begin)
                units = unit_ref[p, begin : begin + size, :]
                along_unit = jnp.sum(units * backs_sum[0:size], axis=-1, keepdims=True)
                grad_rows[p * LP + begin : p * LP + begin + size, :] = (
                    backs_sum[0:size] - units * along_unit
                ) * norm_ref[p, begin : begin + size, :]
        ready = group[-1] + 1
        until = rows if ready == held_count else ready * LP // 16 * 16
        embed_grads[mp, sent_rows:until, :] = grad_rows[sent_rows:until, :].astype(BF16)
        piece = (sent_rows, until - sent_rows)
        pieces.append(piece)
        sent_rows = until
        cut = embed_grads.at[mp, pl.ds(piece[0], piece[1])]
        at = len(pieces) - 1
        for dx in range(1, chips):
            gchip_copies[dx].append(
                start(
                    remote(
                        cut,
                        cut,
                        gchip_sem.at[0, dx, at],
                        gchip_sem.at[1, dx, at],
                        {"mp": mp_at(dx, core)},
                    )
                )
            )
        forward(mp, piece, 0)

    acc[...] = weigh(mp)
    for copy in gpair_copies[0]:
        copy.wait_recv()
    acc[...] += weigh(mp_at(0, other))
    for dx in range(1, chips):
        source = ((chip - dx + chips) % chips) * 2 + core
        for at, piece in enumerate(pieces):
            gchip_copies[dx][at].wait_recv()
            forward(source, piece, dx)
        acc[...] += weigh(source)
    for dx in range(1, chips):
        for copy in gpair_copies[dx]:
            copy.wait_recv()
        acc[...] += weigh(((chip - dx + chips) % chips) * 2 + other)

    share = part_send.shape[1]
    part_send[...] = jnp.transpose(acc[...]).astype(BF16).reshape(n_dp, share, DIM)
    part_copies = []
    for d in range(1, n_dp):
        to = (dp + d) % n_dp
        part_copies.append(
            start(
                remote(
                    part_send.at[to],
                    part_recv.at[d],
                    part_sem.at[0, d],
                    part_sem.at[1, d],
                    {"dp": to},
                )
            )
        )
    whole = part_send[dp].astype(F32)
    for d in range(1, n_dp):
        part_copies[d - 1].wait_recv()
        whole = whole + part_recv[d].astype(F32)
    final[...] = whole.astype(BF16)
    final_copies = []
    for d in range(1, n_dp):
        final_copies.append(
            start(
                remote(
                    final,
                    grad_out.at[dp],
                    final_sem.at[0, d],
                    final_sem.at[1, d],
                    {"dp": (dp + d) % n_dp},
                )
            )
        )
    own_out = pltpu.make_async_copy(final, grad_out.at[dp], out_sem)
    own_out.start()

    for copy in score_copies:
        copy.wait_recv()
    for v in range(slots):
        s, c = v // cap, v % cap
        own_scores[v : v + 1, :] = slot_scores[s, pl.ds(c * n_dp + dp, 1), :]
    by_slot = own_scores[:, 0:n_q]
    for k in range(chosen.shape[0]):
        picked[k : k + 1, :] = jnp.sum(
            jnp.where(slot_row == chosen[k : k + 1, :], by_slot, 0.0), axis=0, keepdims=True
        )
    scores_write = pltpu.make_async_copy(picked, scores_out, scores_sem)
    scores_write.start()
    for copy in pending:
        copy.wait_send()

    def sent(at, carry):
        source = at * sides + side
        for part in range(PARTS):

            @pl.when((at <= line) & (line < lines - 1))
            def _():
                step_right(source, part).wait_send()

            @pl.when((at >= line) & (line > 0))
            def _():
                step_left(source, part).wait_send()

            if sides == 2:
                step_side(source, part).wait_send()
        return carry

    lax.fori_loop(0, lines, sent, 0)
    own_out.wait()
    scores_write.wait()
    for copy in final_copies:
        copy.wait_recv()


def finish(scores, grad, scores_out, grad_out):
    scores_out[...] = scores[...]
    grad_out[...] = grad[...].astype(F32)


def on_device(sizes, states, proj, queries, lengths, slot_passage, candidates, teacher):
    n_dp, n_mp, held_count, cap, n_q = sizes
    width = states.shape[1]
    rows = held_count * LP
    padded = (LP + 15) // 16 * 16
    pairs = n_dp * cap
    share = width // n_dp
    query_rows = n_q * LQ
    chips = n_mp // 2
    vmem = pl.BlockSpec(memory_space=pltpu.VMEM)
    smem = pl.BlockSpec(memory_space=pltpu.SMEM)
    hbm = pl.BlockSpec(memory_space=pl.ANY)
    scores, grad = pl.pallas_call(
        functools.partial(kernel, sizes),
        out_shape=(
            jax.ShapeDtypeStruct(candidates.shape[::-1], F32),
            jax.ShapeDtypeStruct((n_dp, share, DIM), BF16),
        ),
        in_specs=[smem, smem, hbm, hbm, hbm, vmem, vmem],
        out_specs=(hbm, hbm),
        scratch_shapes=[
            pltpu.VMEM((n_mp, rows, width), BF16),
            pltpu.VMEM((width, DIM), BF16),
            pltpu.VMEM((chips, rows, DIM), F32),
            pltpu.VMEM((chips, rows, DIM), F32),
            pltpu.VMEM((chips, rows, DIM), F32),
            pltpu.VMEM((chips, rows, DIM), BF16),
            pltpu.VMEM((chips, rows, DIM), BF16),
            pltpu.VMEM((rows, DIM), F32),
            pltpu.VMEM((held_count, padded, DIM), F32),
            pltpu.VMEM((held_count, padded, DIM), F32),
            pltpu.VMEM((held_count, padded, LANES), F32),
            pltpu.VMEM((held_count, padded, DIM), BF16),
            pltpu.VMEM((n_dp, query_rows, DIM), BF16),
            pltpu.VMEM((n_dp, query_rows, DIM), BF16),
            pltpu.VMEM((pairs, padded, query_rows), F32),
            pltpu.VMEM((pairs, query_rows), F32),
            pltpu.VMEM((pairs, query_rows), F32),
            pltpu.VMEM((pairs, LANES), F32),
            pltpu.VMEM((n_dp, pairs, LANES), F32),
            pltpu.VMEM((n_dp, pairs, LANES), F32),
            pltpu.VMEM((n_dp, pairs, LANES), F32),
            pltpu.VMEM((n_dp, n_dp, LANES), F32),
            pltpu.VMEM((pairs, padded, DIM), F32),
            pltpu.VMEM((rows, DIM), F32),
            pltpu.VMEM((n_mp, rows, DIM), BF16),
            pltpu.VMEM((DIM, width), F32),
            pltpu.VMEM((n_dp, share, DIM), BF16),
            pltpu.VMEM((n_dp, share, DIM), BF16),
            pltpu.VMEM((share, DIM), BF16),
            pltpu.SemaphoreType.DMA((n_mp,)),
            pltpu.SemaphoreType.DMA,
            pltpu.SemaphoreType.DMA,
            pltpu.SemaphoreType.DMA((n_dp, PARTS)),
            pltpu.SemaphoreType.DMA((2, chips)),
            pltpu.SemaphoreType.DMA((2, chips)),
            pltpu.SemaphoreType.DMA((2, n_dp, PARTS)),
            pltpu.SemaphoreType.DMA((2, n_dp, PARTS)),
            pltpu.SemaphoreType.DMA((2, n_dp)),
            pltpu.SemaphoreType.DMA((2, n_dp)),
            pltpu.SemaphoreType.DMA((2, n_dp)),
            pltpu.SemaphoreType.DMA((2, chips, held_count)),
            pltpu.SemaphoreType.DMA((2, chips, held_count)),
            pltpu.SemaphoreType.DMA((2, n_dp)),
            pltpu.SemaphoreType.DMA((2, n_dp)),
            pltpu.SemaphoreType.DMA,
            pltpu.VMEM(candidates.shape[::-1], F32),
            pltpu.SemaphoreType.DMA,
        ],
        compiler_params=pltpu.CompilerParams(
            collective_id=0, has_side_effects=True, vmem_limit_bytes=62 * 1024 * 1024
        ),
    )(
        lengths,
        slot_passage.reshape(n_dp, cap).T,
        states.reshape(n_mp, rows, width),
        proj,
        queries,
        candidates.T,
        teacher.T,
    )
    scores, grad = pl.pallas_call(
        finish,
        out_shape=(
            jax.ShapeDtypeStruct(scores.shape, F32),
            jax.ShapeDtypeStruct((width, DIM), F32),
        ),
        in_specs=[vmem, vmem],
        out_specs=(vmem, vmem),
    )(scores, grad.reshape(width, DIM))
    return scores.T, grad


def solution(mesh):
    n_dp, n_mp = mesh.shape["dp"], mesh.shape["mp"]

    def whole(states, proj, queries, lengths, slot_passage, candidates, teacher):
        devices = n_dp * n_mp
        sizes = (
            n_dp,
            n_mp,
            lengths.shape[0] // devices,
            slot_passage.shape[3],
            candidates.shape[0] // devices,
        )
        return jax.shard_map(
            functools.partial(on_device, sizes),
            mesh=mesh,
            in_specs=(
                P("dp", "mp"),
                P("mp", None),
                P(("dp", "mp"), None),
                P(("dp", "mp")),
                P("dp", "mp", None, None),
                P(("dp", "mp"), None),
                P(("dp", "mp"), None),
            ),
            out_specs=(P(("dp", "mp"), None), P("mp", None)),
            check_vma=False,
        )(states, proj, queries, lengths, slot_passage, candidates, teacher)

    return whole
```

```python
import functools

import jax
import jax.numpy as jnp
from jax import lax
from jax.experimental import pallas as pl
from jax.experimental.pallas import tpu as pltpu
from jax.sharding import PartitionSpec as P

DIM = 128
LQ = 32
LP = 180
LANES = 128
PARTS = 2
ADD_CUTS = 2
ADD_UNROLL = 4
LOG2E = 1.4426950408889634
DEAD = -1e30

smooth_tau = 0.0625
loss_scale = 1024.0
norm_eps = 1e-06

MESH = pl.DeviceIdType.MESH
HIGHEST = lax.Precision.HIGHEST
F32 = jnp.float32
BF16 = jnp.bfloat16


def remote(src, dst, send, recv, where):
    return pltpu.make_async_remote_copy(
        src_ref=src, dst_ref=dst, send_sem=send, recv_sem=recv, device_id=where, device_id_type=MESH
    )


def kernel(
    sizes,
    lengths,
    selected,
    states,
    proj,
    queries,
    candidates,
    teacher,
    scores_out,
    grad_out,
    held,
    proj_ref,
    pair_send,
    pair_recv,
    chip_part,
    chip_send,
    chip_recv,
    embed,
    unit_ref,
    norm_ref,
    bias_ref,
    vectors,
    raw_queries,
    query_vecs,
    powered,
    totals,
    scale_ref,
    own_scores,
    marks,
    marks_by_slot,
    slot_scores,
    shares,
    backs,
    grad_rows,
    embed_grads,
    acc,
    part_send,
    part_recv,
    final,
    load_sem,
    own_sem,
    proj_sem,
    left_sem,
    pair_sem,
    chip_sem,
    row_sem,
    side_sem,
    mark_sem,
    share_sem,
    score_sem,
    gpair_sem,
    gchip_sem,
    part_sem,
    final_sem,
    out_sem,
    picked,
    scores_sem,
):
    n_dp, n_mp, held_count, cap, n_q = sizes
    chips = n_mp // 2
    sides = 2 if n_dp % 2 == 0 else 1
    lines = n_dp // sides
    rows = held_count * LP
    padded = vectors.shape[1]
    slots = n_dp * cap
    dp = lax.axis_index("dp")
    mp = lax.axis_index("mp")
    chip, core = mp // 2, mp % 2
    other = 1 - core
    line, side = dp // sides, dp % sides

    barrier = pltpu.get_barrier_semaphore()
    for d in range(1, n_dp):
        pl.semaphore_signal(
            barrier, inc=1, device_id={"dp": (dp + d) % n_dp}, device_id_type=MESH
        )
    for d in range(1, n_mp):
        pl.semaphore_signal(
            barrier, inc=1, device_id={"mp": (mp + d) % n_mp}, device_id_type=MESH
        )

    def mp_at(dx, which):
        return ((chip + dx) % chips) * 2 + which

    proj_load = pltpu.make_async_copy(proj, proj_ref, proj_sem)
    proj_load.start()
    order = []
    for dx in range(1, chips):
        order += [mp_at(dx, other), mp_at(dx, core)]
    order += [mp_at(0, other), mp_at(0, core)]
    loads = []
    for at, block in enumerate(order):
        copy = pltpu.make_async_copy(states.at[block], held.at[block], load_sem.at[at])
        copy.start()
        loads.append(copy)
    own_load = pltpu.make_async_copy(queries, raw_queries.at[dp], own_sem)
    own_load.start()

    pending = []

    def start(copy):
        copy.start()
        pending.append(copy)
        return copy

    half = queries.shape[0] // PARTS

    def rows_of(part):
        return pl.ds(part * half, half)

    def step_right(source, part, own=False):
        there = raw_queries.at[source, rows_of(part)]
        return remote(
            queries.at[rows_of(part)] if own else there,
            there,
            row_sem.at[0, source, part],
            row_sem.at[1, source, part],
            {"dp": jnp.minimum(line + 1, lines - 1) * sides + side},
        )

    def step_left(source, part, own=False):
        there = raw_queries.at[source, rows_of(part)]
        return remote(
            queries.at[rows_of(part)] if own else there,
            there,
            left_sem.at[source, part],
            row_sem.at[1, source, part],
            {"dp": jnp.maximum(line - 1, 0) * sides + side},
        )

    def step_side(source, part, own=False):
        there = raw_queries.at[source, rows_of(part)]
        return remote(
            queries.at[rows_of(part)] if own else there,
            there,
            side_sem.at[0, source, part],
            side_sem.at[1, source, part],
            {"dp": line * sides + (1 - side)},
        )

    pl.semaphore_wait(barrier, n_dp + n_mp - 2)
    for part in range(PARTS):

        @pl.when(line < lines - 1)
        def _():
            step_right(dp, part, True).start()

        @pl.when(line > 0)
        def _():
            step_left(dp, part, True).start()

    for part in range(PARTS):
        if sides == 2:
            step_side(dp, part, True).start()

    partner = {"mp": mp_at(0, other)}
    pair_copies, chip_copies = {}, {}

    def send_pair(dx):
        pair_copies[dx] = start(
            remote(
                pair_send.at[dx],
                pair_recv.at[dx],
                pair_sem.at[0, dx],
                pair_sem.at[1, dx],
                partner,
            )
        )

    def partial(at):
        loads[at].wait()
        return jnp.dot(held[order[at]], proj_ref[...], preferred_element_type=F32)

    def hop(k, parts):
        for part in parts:

            @pl.when(line >= k)
            def _():
                source = (line - k) * sides + side
                copy = step_right(source, part)
                copy.wait_recv()

                @pl.when(line < lines - 1)
                def _():
                    copy.start()

                if sides == 2:
                    step_side(source, part).start()

            @pl.when(line + k < lines)
            def _():
                source = (line + k) * sides + side
                copy = step_left(source, part)
                copy.wait_recv()

                @pl.when(line > 0)
                def _():
                    copy.start()

                if sides == 2:
                    step_side(source, part).start()

    def prepare(r):
        values = raw_queries[r].astype(F32)
        query_vecs[r] = (
            values / jnp.sqrt(jnp.sum(values * values, axis=-1, keepdims=True) + norm_eps)
        ).astype(BF16)

    def score(r):
        rows_r = query_vecs[r]
        for c in range(cap):
            pair = r * cap + c
            p = selected[c, r]
            similar = lax.dot_general(
                vectors[p], rows_r, (((1,), (1,)), ((), ())), preferred_element_type=F32
            )
            dead = jnp.concatenate([bias_ref[p]] * (similar.shape[1] // LANES), axis=1)
            grown = jnp.exp2(similar * (LOG2E / smooth_tau) + dead)
            powered[pair] = grown
            totals[pl.ds(c * n_dp + r, 1), :] = jnp.sum(grown, axis=0, keepdims=True)

    def along_line(k, body):
        def one(j, carry):
            at = line - k + 2 * k * j

            @pl.when((at >= 0) & (at < lines))
            def _():
                body(at)

            return carry

        lax.fori_loop(0, 1 if k == 0 else 2, one, 0)

    def line_prepare(k):
        along_line(k, lambda at: prepare(at * sides + side))

    def side_arrives(k):
        def body(at):
            source = at * sides + 1 - side
            for part in range(PARTS):
                step_side(source, part).wait_recv()
            prepare(source)
            score(source)

        if sides == 2:
            along_line(k, body)

    proj_load.wait()
    for dx in range(1, chips):
        pair_send[dx] = partial(2 * dx - 2)
        send_pair(dx)
        chip_part[dx] = partial(2 * dx - 1)
    for dx in range(1, chips):
        pair_copies[dx].wait_recv()
        chip_send[dx] = (chip_part[dx] + pair_recv[dx]).astype(BF16)
        chip_copies[dx] = start(
            remote(
                chip_send.at[dx],
                chip_recv.at[dx],
                chip_sem.at[0, dx],
                chip_sem.at[1, dx],
                {"mp": mp_at(dx, core)},
            )
        )
    hop(1, (0,))
    pair_send[0] = partial(n_mp - 2)
    send_pair(0)
    hop(1, (1,))
    embed[...] = partial(n_mp - 1)


    target = jnp.exp(teacher[...])
    target = target / jnp.sum(target, axis=0, keepdims=True)
    chosen = candidates[...]
    slot_row = lax.broadcasted_iota(jnp.int32, (slots, n_q), 0)
    by_slot = jnp.full((slots, n_q), -1.0, F32)
    for k in range(chosen.shape[0]):
        by_slot = jnp.where(slot_row == chosen[k : k + 1, :], target[k : k + 1, :], by_slot)
    marks[dp] = jnp.full((slots, LANES), -1.0, F32)
    marks[dp, :, 0:n_q] = by_slot
    row_at = lax.broadcasted_iota(jnp.int32, (padded, LANES), 0)
    for p in range(held_count):
        bias_ref[p] = jnp.where(row_at < lengths[p], 0.0, DEAD)
    own_load.wait()
    line_prepare(0)
    hop(2, (0,))
    hop(2, (1,))
    pair_copies[0].wait_recv()
    embed[...] += pair_recv[0]
    mark_copies = []
    for d in range(1, n_dp):
        there = {"dp": (dp + d) % n_dp}
        mark_copies.append(
            start(
                remote(marks.at[dp], marks.at[dp], mark_sem.at[0, d], mark_sem.at[1, d], there)
            )
        )
    line_prepare(1)
    for k in range(3, lines - 1):
        hop(k, range(PARTS))
        line_prepare(k - 1)
    total = embed[...]
    for dx in range(1, chips):
        chip_copies[dx].wait_recv()
        total = total + chip_recv[dx].astype(F32)
    embed[...] = total
    for p in range(held_count):
        piece = embed[p * LP : (p + 1) * LP, :]
        norms = jnp.sqrt(jnp.sum(piece * piece, axis=-1, keepdims=True) + norm_eps)
        units = piece / norms
        unit_ref[p, 0:LP, :] = units
        unit_ref[p, LP:padded, :] = jnp.zeros((padded - LP, DIM), F32)
        norm_ref[p, 0:LP, :] = jnp.broadcast_to(1.0 / norms, (LP, DIM))
        vectors[p] = unit_ref[p].astype(BF16)

    def line_score(k):
        along_line(k, lambda at: score(at * sides + side))

    early = max(lines - 2, 0)
    for k in range(early):
        line_score(k)
    if lines > 3:
        hop(lines - 1, range(PARTS))
        line_prepare(lines - 2)
    side_arrives(0)
    if lines > 2:
        line_score(lines - 2)
    if lines > 1:
        line_prepare(lines - 1)
    if early < lines - 1 or lines == 1:
        line_score(lines - 1)
    for copy in mark_copies:
        copy.wait_recv()
    for v in range(slots):
        s, c = v // cap, v % cap
        marks_by_slot[s, c * n_dp : (c + 1) * n_dp, :] = marks[:, v, :]
    for k in range(1, lines):
        side_arrives(k)

    spread = (
        lax.broadcasted_iota(jnp.int32, (n_q * LQ, LANES), 0) // LQ
        == lax.broadcasted_iota(jnp.int32, (n_q * LQ, LANES), 1)
    ).astype(BF16)

    def split(value):
        high = value.astype(BF16)
        rest = value - high.astype(F32)
        middle = rest.astype(BF16)
        low = (rest - middle.astype(F32)).astype(BF16)
        return jnp.concatenate([high, middle, low], axis=0)

    def joined(value):
        return value[0:slots] + value[slots : 2 * slots] + value[2 * slots : 3 * slots]

    sums = totals[...]
    own_slots = smooth_tau * joined(
        jnp.dot(split(jnp.log(sums)), spread, preferred_element_type=F32)
    )
    own_marks = marks_by_slot[dp]
    student = jnp.where(own_marks >= 0.0, jnp.exp(own_slots), 0.0)
    mine = student[0:n_dp, :]
    for c in range(1, cap):
        mine = mine + student[c * n_dp : (c + 1) * n_dp, :]
    shares[dp] = mine
    share_copies, score_copies = [], []
    for d in range(1, n_dp):
        there = {"dp": (dp + d) % n_dp}
        share_copies.append(
            start(
                remote(
                    shares.at[dp], shares.at[dp], share_sem.at[0, d], share_sem.at[1, d], there
                )
            )
        )
    slot_scores[dp] = own_slots
    per_sum = loss_scale / sums
    for copy in share_copies:
        copy.wait_recv()

    whole = jnp.sum(shares[...], axis=0)
    whole = jnp.concatenate([whole] * cap, axis=0)
    slot_grad = jnp.where(own_marks >= 0.0, student / whole - own_marks, 0.0)
    scale_ref[...] = (
        joined(
            lax.dot_general(
                split(slot_grad), spread, (((1,), (1,)), ((), ())), preferred_element_type=F32
            )
        )
        * per_sum
    )
    def back(r, carry):
        rows_r = query_vecs[r]
        for c in range(cap):
            pair = r * cap + c
            coefficient = (powered[pair] * scale_ref[pl.ds(c * n_dp + r, 1), :]).astype(BF16)
            backs[pair] = jnp.dot(coefficient, rows_r, preferred_element_type=F32)
        return carry

    lax.fori_loop(0, n_dp, back, 0, unroll=8)

    for d in range(1, n_dp):
        there = {"dp": (dp + d) % n_dp}
        score_copies.append(
            start(
                remote(
                    slot_scores.at[dp],
                    slot_scores.at[dp],
                    score_sem.at[0, d],
                    score_sem.at[1, d],
                    there,
                )
            )
        )

    def weigh(block):
        return lax.dot_general(
            embed_grads[block], held[block], (((0,), (0,)), ((), ())), preferred_element_type=F32
        )

    gchip_copies = [[] for _ in range(chips)]
    gpair_copies = [[] for _ in range(chips)]

    def forward(source, piece, dx):
        begin, size = piece
        cut = embed_grads.at[source, pl.ds(begin, size)]
        at = len(gpair_copies[dx])
        gpair_copies[dx].append(
            start(remote(cut, cut, gpair_sem.at[0, dx, at], gpair_sem.at[1, dx, at], partner))
        )

    pieces = []
    ready, sent_rows = 0, 0
    step = max(8, padded // ADD_CUTS)
    while ready < held_count:
        group = range(ready, min(ready + 2, held_count))
        grown_parts = [[] for _ in group]
        for cut in range(0, padded, step):

            def add(pair, sofar):
                piece = backs[pair, cut : cut + step, :]
                which = selected[pair % cap, pair // cap]
                return tuple(
                    now + jnp.where(which == p, piece, 0.0) for now, p in zip(sofar, group)
                )

            zero = jnp.zeros((step, DIM), F32)
            done = lax.fori_loop(0, slots, add, tuple(zero for _ in group), unroll=ADD_UNROLL)
            for keep, value in zip(grown_parts, done):
                keep.append(value)
        for keep, p in zip(grown_parts, group):
            for at, value in enumerate(keep):
                backs_sum = value
                begin = at * step
                size = min(step, LP - begin)
                units = unit_ref[p, begin : begin + size, :]
                along_unit = jnp.sum(units * backs_sum[0:size], axis=-1, keepdims=True)
                grad_rows[p * LP + begin : p * LP + begin + size, :] = (
                    backs_sum[0:size] - units * along_unit
                ) * norm_ref[p, begin : begin + size, :]
        ready = group[-1] + 1
        until = rows if ready == held_count else ready * LP // 16 * 16
        embed_grads[mp, sent_rows:until, :] = grad_rows[sent_rows:until, :].astype(BF16)
        piece = (sent_rows, until - sent_rows)
        pieces.append(piece)
        sent_rows = until
        cut = embed_grads.at[mp, pl.ds(piece[0], piece[1])]
        at = len(pieces) - 1
        for dx in range(1, chips):
            gchip_copies[dx].append(
                start(
                    remote(
                        cut,
                        cut,
                        gchip_sem.at[0, dx, at],
                        gchip_sem.at[1, dx, at],
                        {"mp": mp_at(dx, core)},
                    )
                )
            )
        forward(mp, piece, 0)

    acc[...] = weigh(mp)
    for copy in gpair_copies[0]:
        copy.wait_recv()
    acc[...] += weigh(mp_at(0, other))
    for dx in range(1, chips):
        source = ((chip - dx + chips) % chips) * 2 + core
        for at, piece in enumerate(pieces):
            gchip_copies[dx][at].wait_recv()
            forward(source, piece, dx)
        acc[...] += weigh(source)
    for dx in range(1, chips):
        for copy in gpair_copies[dx]:
            copy.wait_recv()
        acc[...] += weigh(((chip - dx + chips) % chips) * 2 + other)

    share = part_send.shape[1]
    part_send[...] = jnp.transpose(acc[...]).astype(BF16).reshape(n_dp, share, DIM)
    zigzag = sorted(range(1, n_dp), key=lambda d: (min(d, n_dp - d), d))
    part_copies = []
    for d in zigzag:
        to = (dp + d) % n_dp
        part_copies.append(
            start(
                remote(
                    part_send.at[to],
                    part_recv.at[d],
                    part_sem.at[0, d],
                    part_sem.at[1, d],
                    {"dp": to},
                )
            )
        )
    whole = part_send[dp].astype(F32)
    for d in range(1, n_dp):
        part_copies[zigzag.index(d)].wait_recv()
        whole = whole + part_recv[d].astype(F32)
    final[...] = whole.astype(BF16)
    final_copies = []
    for d in range(1, n_dp):
        final_copies.append(
            start(
                remote(
                    final,
                    grad_out.at[dp],
                    final_sem.at[0, d],
                    final_sem.at[1, d],
                    {"dp": (dp + d) % n_dp},
                )
            )
        )
    own_out = pltpu.make_async_copy(final, grad_out.at[dp], out_sem)
    own_out.start()

    for copy in score_copies:
        copy.wait_recv()
    for v in range(slots):
        s, c = v // cap, v % cap
        own_scores[v : v + 1, :] = slot_scores[s, pl.ds(c * n_dp + dp, 1), :]
    by_slot = own_scores[:, 0:n_q]
    for k in range(chosen.shape[0]):
        picked[k : k + 1, :] = jnp.sum(
            jnp.where(slot_row == chosen[k : k + 1, :], by_slot, 0.0), axis=0, keepdims=True
        )
    scores_write = pltpu.make_async_copy(picked, scores_out, scores_sem)
    scores_write.start()
    for copy in pending:
        copy.wait_send()

    def sent(at, carry):
        source = at * sides + side
        for part in range(PARTS):

            @pl.when((at <= line) & (line < lines - 1))
            def _():
                step_right(source, part).wait_send()

            @pl.when((at >= line) & (line > 0))
            def _():
                step_left(source, part).wait_send()

            if sides == 2:
                step_side(source, part).wait_send()
        return carry

    lax.fori_loop(0, lines, sent, 0)
    own_out.wait()
    scores_write.wait()
    for copy in final_copies:
        copy.wait_recv()


def finish(scores, grad, scores_out, grad_out):
    scores_out[...] = scores[...]
    grad_out[...] = grad[...].astype(F32)


def on_device(sizes, states, proj, queries, lengths, slot_passage, candidates, teacher):
    n_dp, n_mp, held_count, cap, n_q = sizes
    width = states.shape[1]
    rows = held_count * LP
    padded = (LP + 15) // 16 * 16
    pairs = n_dp * cap
    share = width // n_dp
    query_rows = n_q * LQ
    chips = n_mp // 2
    vmem = pl.BlockSpec(memory_space=pltpu.VMEM)
    smem = pl.BlockSpec(memory_space=pltpu.SMEM)
    hbm = pl.BlockSpec(memory_space=pl.ANY)
    scores, grad = pl.pallas_call(
        functools.partial(kernel, sizes),
        out_shape=(
            jax.ShapeDtypeStruct(candidates.shape[::-1], F32),
            jax.ShapeDtypeStruct((n_dp, share, DIM), BF16),
        ),
        in_specs=[smem, smem, hbm, hbm, hbm, vmem, vmem],
        out_specs=(hbm, hbm),
        scratch_shapes=[
            pltpu.VMEM((n_mp, rows, width), BF16),
            pltpu.VMEM((width, DIM), BF16),
            pltpu.VMEM((chips, rows, DIM), F32),
            pltpu.VMEM((chips, rows, DIM), F32),
            pltpu.VMEM((chips, rows, DIM), F32),
            pltpu.VMEM((chips, rows, DIM), BF16),
            pltpu.VMEM((chips, rows, DIM), BF16),
            pltpu.VMEM((rows, DIM), F32),
            pltpu.VMEM((held_count, padded, DIM), F32),
            pltpu.VMEM((held_count, padded, DIM), F32),
            pltpu.VMEM((held_count, padded, LANES), F32),
            pltpu.VMEM((held_count, padded, DIM), BF16),
            pltpu.VMEM((n_dp, query_rows, DIM), BF16),
            pltpu.VMEM((n_dp, query_rows, DIM), BF16),
            pltpu.VMEM((pairs, padded, query_rows), F32),
            pltpu.VMEM((pairs, query_rows), F32),
            pltpu.VMEM((pairs, query_rows), F32),
            pltpu.VMEM((pairs, LANES), F32),
            pltpu.VMEM((n_dp, pairs, LANES), F32),
            pltpu.VMEM((n_dp, pairs, LANES), F32),
            pltpu.VMEM((n_dp, pairs, LANES), F32),
            pltpu.VMEM((n_dp, n_dp, LANES), F32),
            pltpu.VMEM((pairs, padded, DIM), F32),
            pltpu.VMEM((rows, DIM), F32),
            pltpu.VMEM((n_mp, rows, DIM), BF16),
            pltpu.VMEM((DIM, width), F32),
            pltpu.VMEM((n_dp, share, DIM), BF16),
            pltpu.VMEM((n_dp, share, DIM), BF16),
            pltpu.VMEM((share, DIM), BF16),
            pltpu.SemaphoreType.DMA((n_mp,)),
            pltpu.SemaphoreType.DMA,
            pltpu.SemaphoreType.DMA,
            pltpu.SemaphoreType.DMA((n_dp, PARTS)),
            pltpu.SemaphoreType.DMA((2, chips)),
            pltpu.SemaphoreType.DMA((2, chips)),
            pltpu.SemaphoreType.DMA((2, n_dp, PARTS)),
            pltpu.SemaphoreType.DMA((2, n_dp, PARTS)),
            pltpu.SemaphoreType.DMA((2, n_dp)),
            pltpu.SemaphoreType.DMA((2, n_dp)),
            pltpu.SemaphoreType.DMA((2, n_dp)),
            pltpu.SemaphoreType.DMA((2, chips, held_count)),
            pltpu.SemaphoreType.DMA((2, chips, held_count)),
            pltpu.SemaphoreType.DMA((2, n_dp)),
            pltpu.SemaphoreType.DMA((2, n_dp)),
            pltpu.SemaphoreType.DMA,
            pltpu.VMEM(candidates.shape[::-1], F32),
            pltpu.SemaphoreType.DMA,
        ],
        compiler_params=pltpu.CompilerParams(
            collective_id=0, has_side_effects=True, vmem_limit_bytes=62 * 1024 * 1024
        ),
    )(
        lengths,
        slot_passage.reshape(n_dp, cap).T,
        states.reshape(n_mp, rows, width),
        proj,
        queries,
        candidates.T,
        teacher.T,
    )
    scores, grad = pl.pallas_call(
        finish,
        out_shape=(
            jax.ShapeDtypeStruct(scores.shape, F32),
            jax.ShapeDtypeStruct((width, DIM), F32),
        ),
        in_specs=[vmem, vmem],
        out_specs=(vmem, vmem),
    )(scores, grad.reshape(width, DIM))
    return scores.T, grad


def solution(mesh):
    n_dp, n_mp = mesh.shape["dp"], mesh.shape["mp"]

    def whole(states, proj, queries, lengths, slot_passage, candidates, teacher):
        devices = n_dp * n_mp
        sizes = (
            n_dp,
            n_mp,
            lengths.shape[0] // devices,
            slot_passage.shape[3],
            candidates.shape[0] // devices,
        )
        return jax.shard_map(
            functools.partial(on_device, sizes),
            mesh=mesh,
            in_specs=(
                P("dp", "mp"),
                P("mp", None),
                P(("dp", "mp"), None),
                P(("dp", "mp")),
                P("dp", "mp", None, None),
                P(("dp", "mp"), None),
                P(("dp", "mp"), None),
            ),
            out_specs=(P(("dp", "mp"), None), P("mp", None)),
            check_vma=False,
        )(states, proj, queries, lengths, slot_passage, candidates, teacher)

    return whole
```
